32 devices in a mesh: groups: 2 (over y), seq: 4 (over z), section: 2 (over x), chan: 2 (over core).
Axes of the slice: x: 2, y: 2, z: 4, core: 2. Of those that a mesh axis runs over, the one named last changes fastest.
Arguments:
- base_codes: int32 [131072], P(('groups', 'seq', 'section')), parts along dimension 0, may hold values from 0 to 3
- stem_weight: bfloat16 [64, 768], replicated, as said below
- conv_gain: float32 [768], replicated, may hold values from 0.1 to 1.9
- dilated_conv_weight: bfloat16 [3, 768, 768], P(None, None, 'chan'), may hold values from -0.125 to 0.125
- widen_weight: bfloat16 [768, 1536], P(None, 'chan'), may hold values from -0.21875 to 0.21875
- token_gain: float32 [1536], replicated, may hold values from 0.1 to 1.9
- proj_weight: bfloat16 [1536, 256], replicated, may hold values from -0.15625 to 0.15625
- dist_weight: float32 [128], replicated, may hold values from -4 to 4
- pair_weight_one: bfloat16 [3, 3, 128, 128], P(None, None, None, 'chan'), may hold values from -0.1875 to 0.1875
- pair_weight_two: bfloat16 [3, 3, 128, 128], P(None, None, None, 'chan'), may hold values from -0.1875 to 0.1875
Outputs:
- fine_features: bfloat16 [4096, 1536], P(('groups', 'seq', 'section'), 'chan'), parts along dimension 0
- pair_map: bfloat16 [128, 64, 32], P('chan', ('groups', 'seq'), 'section'), parts along dimension 1
The draws below stay inside these ranges and needn't reach their ends.
There are 2 independent parts, one for each index of `groups`. The reference program is written for one: setup_inputs(seed, part) draws one part's arguments, and reference() takes and returns one part's arrays. A program takes and returns all parts, laid end to end along the dimension named above; an argument that names none is the same for every part. Nothing has to cross between parts.
Inputs may be any that keep to these rules, and one draw needn't show every extreme that they name: Each entry of stem_weight is under 9 / sqrt(16) in magnitude.
All inputs are finite; a program needn't handle non-finite values.
Results may differ from the reference program's by a relative error of at most 0.015.
Values may be sent and summed in bfloat16 or wider, within the bound.
No kernel may reach another device: no remote copies, remote signals or barrier semaphores. Data moves between devices by JAX's collectives and lax.ppermute only.
A program may use at most 64 MiB of HBM per device.

```python
import math
import jax
import jax.numpy as jnp
from jax import lax

C1 = 768
C2 = 1536
PC = 128
PATCH = 16
POOL = 64
DILATION_ROWS = 4
TOKENS = 32
BASES = 65536


def draw_stem_weight(key, part):
    key_base = jax.random.fold_in(key, 11)
    key_scale = jax.random.fold_in(key, 12)
    exponent = jax.random.uniform(key_scale, (C1,), jnp.float32)
    column_scale = 0.22 * jnp.exp(exponent * math.log(10.0))
    values = jnp.clip(jax.random.normal(key_base, (4 * PATCH, C1), jnp.float32), -4.0, 4.0)
    return (values * column_scale[None, :] / math.sqrt(PATCH)).astype(jnp.bfloat16)


def place_ends(drawn, stream_key, smallest, high):
    spot = [jax.random.randint(jax.random.fold_in(stream_key, axis), (), 0, length) for axis, length in enumerate(drawn.shape)]
    longest = drawn.shape.index(max(drawn.shape))
    beside = spot[:longest] + [(spot[longest] + 1) % drawn.shape[longest]] + spot[longest + 1:]
    return drawn.at[tuple(spot)].set(smallest).at[tuple(beside)].set(high)


def shard_levels(key, shape, split, low, high):
    def one(dim, blocks):
        draws = jax.random.uniform(jax.random.fold_in(jax.random.fold_in(key, 6), dim), (blocks,), jnp.float32, low / len(split), high / len(split))
        return jnp.repeat(jnp.exp(draws), shape[dim] // blocks).reshape((-1,) + (1,) * (len(shape) - dim - 1))

    level = one(*split[0])
    for cut in split[1:]:
        level = level * one(*cut)
    return level


def gaussian(key, dims, width, most, split=(), kind=jnp.bfloat16):
    drawn = width * jax.random.normal(key, dims, jnp.float32)
    if split:
        drawn = drawn * shard_levels(key, dims, split, -0.22, 0.18)
    return jnp.clip(drawn, -most, most).astype(kind)


def setup_inputs(seed: int = 0, part: int = 0) -> dict:
    seeds = jax.random.split(jax.random.key(seed), 11)
    part_keys = jax.random.split(jax.random.fold_in(seeds[10], part), 11)
    base_codes = place_ends(jax.random.randint(part_keys[0], (BASES,), 0, 4), jax.random.fold_in(part_keys[0], 1), 0, 3).astype(jnp.int32)
    stem_weight = draw_stem_weight(jax.random.fold_in(seeds[10], 71), part)
    conv_gain = jnp.clip(1.0 + 0.18 * jax.random.normal(seeds[2], (C1,), jnp.float32), 0.1, 1.9)
    dilated_conv_weight = gaussian(seeds[3], (3, C1, C1), (3 * C1) ** -0.5, 0.125, ((2, 2),))
    widen_weight = gaussian(seeds[4], (C1, C2), C1 ** -0.5, 0.21875, ((1, 2),))
    token_gain = jnp.clip(1.0 + 0.18 * jax.random.normal(seeds[5], (C2,), jnp.float32), 0.1, 1.9)
    proj_weight = gaussian(seeds[6], (C2, 2 * PC), C2 ** -0.5, 0.15625)
    dist_weight = gaussian(seeds[7], (PC,), 1.0, 4.0, (), jnp.float32)
    pair_weight_one = gaussian(seeds[8], (3, 3, PC, PC), (9 * PC) ** -0.5, 0.1875, ((3, 2),))
    pair_weight_two = gaussian(seeds[9], (3, 3, PC, PC), (9 * PC) ** -0.5, 0.1875, ((3, 2),))
    return {"base_codes": base_codes, "stem_weight": stem_weight, "conv_gain": conv_gain, "dilated_conv_weight": dilated_conv_weight, "widen_weight": widen_weight, "token_gain": token_gain, "proj_weight": proj_weight, "dist_weight": dist_weight, "pair_weight_one": pair_weight_one, "pair_weight_two": pair_weight_two}


epsilon = 1e-06

def row_norm(values, gain):
    mean_square = lax.optimization_barrier(jnp.mean(values * values, axis=1, keepdims=True))
    return values * lax.rsqrt(mean_square + epsilon) * gain

def pair_conv(active, weight):
    padded_rows = jnp.pad(active, ((0, 0), (1, 1), (1, 1)))
    row_len = active.shape[1]
    col_len = active.shape[2]
    total = jnp.zeros((weight.shape[3], row_len, col_len), jnp.float32)
    for shift_row in range(3):
        for shift_col in range(3):
            window = padded_rows[:, shift_row:shift_row + row_len, shift_col:shift_col + col_len].astype(jnp.float32)
            total = total + jnp.einsum('co,crs->ors', weight[shift_row, shift_col].astype(jnp.float32), window)
    return total

def reference(base_codes, stem_weight, conv_gain, dilated_conv_weight, widen_weight, token_gain, proj_weight, dist_weight, pair_weight_one, pair_weight_two):
    count_of_rows = BASES // PATCH
    coded = base_codes.reshape(count_of_rows, PATCH)
    onehot = (coded[:, :, None] == jnp.arange(4, dtype=jnp.int32)[None, None, :]).astype(jnp.bfloat16).reshape(count_of_rows, 4 * PATCH)
    stem_output = jnp.dot(onehot, stem_weight, preferred_element_type=jnp.float32).astype(jnp.bfloat16)
    padded_rows = jnp.pad(stem_output, ((DILATION_ROWS, DILATION_ROWS), (0, 0))).astype(jnp.float32)
    normalized_rows = row_norm(padded_rows, conv_gain).astype(jnp.bfloat16)
    summed_taps = jnp.zeros((count_of_rows, C1), jnp.float32)
    for row_shift_amount in range(3):
        summed_taps = summed_taps + jnp.dot(normalized_rows[row_shift_amount * DILATION_ROWS:row_shift_amount * DILATION_ROWS + count_of_rows], dilated_conv_weight[row_shift_amount], preferred_element_type=jnp.float32)
    tower = (stem_output.astype(jnp.float32) + jax.nn.gelu(summed_taps)).astype(jnp.bfloat16)
    halved = jnp.maximum(tower[0::2], tower[1::2])
    fine_features = jax.nn.gelu(jnp.dot(halved, widen_weight, preferred_element_type=jnp.float32)).astype(jnp.bfloat16)
    token = lax.optimization_barrier(jnp.mean(fine_features.astype(jnp.float32).reshape(TOKENS, POOL, C2), axis=1)).astype(jnp.bfloat16)
    token_norm = row_norm(token.astype(jnp.float32), token_gain).astype(jnp.bfloat16)
    factors = jnp.dot(token_norm, proj_weight, preferred_element_type=jnp.float32).astype(jnp.bfloat16)
    row_factor = factors[:, :PC].astype(jnp.float32)
    col_factor = factors[:, PC:].astype(jnp.float32)
    position = jnp.arange(TOKENS, dtype=jnp.int32)
    distance = jnp.log1p(jnp.abs(position[:, None] - position[None, :]).astype(jnp.float32)) / math.log(TOKENS)
    pair_start = (row_factor.T[:, :, None] * col_factor.T[:, None, :] + dist_weight[:, None, None] * distance[None, :, :]).astype(jnp.bfloat16)
    act_one = jax.nn.gelu(pair_start.astype(jnp.float32)).astype(jnp.bfloat16)
    pair_mid = (pair_start.astype(jnp.float32) + pair_conv(act_one, pair_weight_one)).astype(jnp.bfloat16)
    act_two = jax.nn.gelu(pair_mid.astype(jnp.float32)).astype(jnp.bfloat16)
    pair_map = (pair_mid.astype(jnp.float32) + pair_conv(act_two, pair_weight_two)).astype(jnp.bfloat16)
    return (fine_features, pair_map)
```

```python
import math

import jax
import jax.numpy as jnp
from jax import lax
from jax.sharding import PartitionSpec as P

PC = 128
PATCH = 16
POOL = 64
DILATION_ROWS = 4


epsilon = 1e-06
CHIPS = ("seq", "section")
PART = ("seq", "section", "chan")


def swap(values):
    count = lax.axis_size("chan")
    return lax.ppermute(values, "chan", [(i, count - 1 - i) for i in range(count)])


def row_norm(values, gain):
    mean_square = jnp.mean(values * values, axis=1, keepdims=True)
    return values * lax.rsqrt(mean_square + epsilon) * gain


def in_order(core, own, other, axis):
    first = jnp.where(core == 0, own, other)
    second = jnp.where(core == 0, other, own)
    return jnp.concatenate([first, second], axis=axis)


def pair_conv(active, weight):
    row_len = active.shape[0] - 2
    col_len = active.shape[1] - 2
    total = jnp.zeros((row_len, col_len, weight.shape[3]), jnp.float32)
    for shift_row in range(3):
        for shift_col in range(3):
            window = active[shift_row : shift_row + row_len, shift_col : shift_col + col_len]
            total = total + jnp.einsum(
                "rsc,co->rso",
                window,
                weight[shift_row, shift_col],
                preferred_element_type=jnp.float32,
            )
    return total


def per_device(
    base_codes,
    stem_weight,
    conv_gain,
    dilated_conv_weight,
    widen_weight,
    token_gain,
    proj_weight,
    dist_weight,
    pair_weight_one,
    pair_weight_two,
):
    seq_count = lax.axis_size("seq")
    section_count = lax.axis_size("section")
    core_count = lax.axis_size("chan")
    chip_count = seq_count * section_count
    core = lax.axis_index("chan")
    chip = lax.axis_index(CHIPS)
    last = core_count - 1

    halo = DILATION_ROWS * PATCH
    outgoing = jnp.where(core == 0, base_codes[:halo], base_codes[-halo:])
    pairs = []
    for i in range(chip_count - 1):
        low, high = i * core_count + last, (i + 1) * core_count
        pairs += [(low, high), (high, low)]
    received = lax.ppermute(outgoing, PART, pairs)
    dilated_other = swap(dilated_conv_weight)
    widen_other = swap(widen_weight)
    pair_one_other = swap(pair_weight_one)

    rows = base_codes.shape[0] // PATCH // core_count
    codes = jnp.concatenate([received, base_codes, received])
    codes = lax.dynamic_slice_in_dim(codes, core * rows * PATCH, rows * PATCH + 2 * halo)
    rows_ext = rows + 2 * DILATION_ROWS
    coded = codes.reshape(rows_ext, PATCH)
    place = (chip * core_count + core) * rows - DILATION_ROWS + jnp.arange(rows_ext)
    valid = (place >= 0) & (place < chip_count * core_count * rows)
    onehot = (
        (
            (coded[:, :, None] == jnp.arange(4, dtype=jnp.int32)[None, None, :])
            & valid[:, None, None]
        )
        .astype(jnp.bfloat16)
        .reshape(rows_ext, 4 * PATCH)
    )
    stem = jnp.dot(onehot, stem_weight, preferred_element_type=jnp.float32).astype(jnp.bfloat16)
    normed = row_norm(stem.astype(jnp.float32), conv_gain).astype(jnp.bfloat16)

    def taps(weight):
        total = jnp.zeros((rows, weight.shape[2]), jnp.float32)
        for k in range(3):
            total = total + jnp.dot(
                normed[k * DILATION_ROWS : k * DILATION_ROWS + rows],
                weight[k],
                preferred_element_type=jnp.float32,
            )
        return jax.nn.gelu(total)

    branch = in_order(core, taps(dilated_conv_weight), taps(dilated_other), 1)
    tower = (
        stem[DILATION_ROWS : DILATION_ROWS + rows].astype(jnp.float32) + branch
    ).astype(jnp.bfloat16)
    halved = jnp.maximum(tower[0::2], tower[1::2])

    def widen(weight):
        return jax.nn.gelu(jnp.dot(halved, weight, preferred_element_type=jnp.float32)).astype(
            jnp.bfloat16
        )

    fine_own, fine_other = widen(widen_weight), widen(widen_other)
    fine_features = in_order(core, fine_own, swap(fine_other), 0)
    fine = in_order(core, fine_own, fine_other, 1)
    tok_count = fine.shape[0] // POOL
    token = jnp.mean(
        fine.astype(jnp.float32).reshape(tok_count, POOL, fine.shape[1]), axis=1
    ).astype(jnp.bfloat16)
    token_norm = row_norm(token.astype(jnp.float32), token_gain).astype(jnp.bfloat16)
    factors = jnp.dot(token_norm, proj_weight, preferred_element_type=jnp.float32).astype(
        jnp.bfloat16
    )

    members = chip_count * core_count
    spread = jnp.broadcast_to(factors[None], (members,) + factors.shape)
    every = lax.all_to_all(spread, PART, 0, 0, tiled=True)
    tokens_total = tok_count * members
    every = every.reshape(tokens_total, 2 * PC)

    tile_height = tokens_total // seq_count
    tile_width = tokens_total // section_count
    row_anchor = lax.axis_index("seq") * tile_height
    col_anchor = lax.axis_index("section") * tile_width
    zero_padded = jnp.pad(every, ((2, 2), (0, 0)))
    row_factor = lax.dynamic_slice_in_dim(zero_padded, row_anchor, tile_height + 4, 0)[:, :PC]
    col_factor = lax.dynamic_slice_in_dim(zero_padded, col_anchor, tile_width + 4, 0)[:, PC:]
    row_index = row_anchor - 2 + jnp.arange(tile_height + 4, dtype=jnp.int32)
    col_index = col_anchor - 2 + jnp.arange(tile_width + 4, dtype=jnp.int32)
    gap = jnp.abs(row_index[:, None] - col_index[None, :]).astype(jnp.float32)
    distance = jnp.log1p(gap) / math.log(tokens_total)
    start = (
        row_factor.astype(jnp.float32)[:, None, :] * col_factor.astype(jnp.float32)[None, :, :]
        + distance[:, :, None] * dist_weight[None, None, :]
    ).astype(jnp.bfloat16)
    row_valid = (row_index >= 0) & (row_index < tokens_total)
    col_valid = (col_index >= 0) & (col_index < tokens_total)
    inside = (row_valid[:, None] & col_valid[None, :])[:, :, None]

    def activate(cells, mask):
        return jnp.where(mask, jax.nn.gelu(cells.astype(jnp.float32)), 0.0).astype(jnp.bfloat16)

    weight_one = in_order(core, pair_weight_one, pair_one_other, 3)
    mid = (
        start[1:-1, 1:-1].astype(jnp.float32) + pair_conv(activate(start, inside), weight_one)
    ).astype(jnp.bfloat16)
    act_two = activate(mid, inside[1:-1, 1:-1])
    pair_own = pair_weight_two.shape[3]
    mid_own = lax.dynamic_slice_in_dim(mid[1:-1, 1:-1], core * pair_own, pair_own, 2)
    pair_map = (mid_own.astype(jnp.float32) + pair_conv(act_two, pair_weight_two)).astype(
        jnp.bfloat16
    )
    return (fine_features, pair_map.transpose(2, 0, 1))


def solution(mesh):
    in_specs = (
        P(("groups", "seq", "section")),
        P(),
        P(),
        P(None, None, "chan"),
        P(None, "chan"),
        P(),
        P(),
        P(),
        P(None, None, None, "chan"),
        P(None, None, None, "chan"),
    )
    out_specs = (P(("groups", "seq", "section"), "chan"), P("chan", ("groups", "seq"), "section"))
    return jax.shard_map(
        per_device, mesh=mesh, in_specs=in_specs, out_specs=out_specs, check_vma=False
    )
```

```python
import functools
import math

import jax
import jax.numpy as jnp
from jax import lax
from jax.experimental import pallas as pl
from jax.experimental.pallas import tpu as pltpu
from jax.sharding import PartitionSpec as P

PC = 128
PATCH = 16
POOL = 64
DILATION_ROWS = 4


epsilon = 1e-06
LANES = 128
SUB = 8
CHIPS = ("seq", "section")
PART = ("seq", "section", "chan")
VMEM = pl.BlockSpec(memory_space=pltpu.VMEM)
SMEM = pl.BlockSpec(memory_space=pltpu.SMEM)
HBM = pl.BlockSpec(memory_space=pltpu.HBM)
ANY = pl.BlockSpec(memory_space=pl.ANY)
LIMIT = 16 << 20


def swap(values):
    count = lax.axis_size("chan")
    return lax.ppermute(values, "chan", [(i, count - 1 - i) for i in range(count)])


def dot(a, b):
    return jnp.dot(a, b, preferred_element_type=jnp.float32)


def iota(shape, axis):
    return lax.broadcasted_iota(jnp.int32, shape, axis)


def spread_codes(tiles):
    own_patch = iota((SUB, LANES), 1) // PATCH == iota((SUB, LANES), 0)
    picked = jnp.concatenate(
        [jnp.where(own_patch, t, 0).astype(jnp.float32) for t in tiles], axis=0
    ).astype(jnp.bfloat16)
    width = 4 * PATCH
    gather = (iota((LANES, width), 0) % PATCH == iota((LANES, width), 1) // 4).astype(jnp.bfloat16)
    return dot(picked, gather)


def stem_of(codes, valid, stem_weight, gain):
    base = (iota(codes.shape, 1) % 4).astype(jnp.float32)
    onehot = jnp.where((codes == base) & valid, 1.0, 0.0).astype(jnp.bfloat16)
    stem = dot(onehot, stem_weight).astype(jnp.bfloat16).astype(jnp.float32)
    mean_square = jnp.mean(stem * stem, axis=1, keepdims=True)
    normed = (stem * lax.rsqrt(mean_square + epsilon) * gain).astype(jnp.bfloat16)
    return stem, normed


def in_lanes(rows):
    return jnp.concatenate([rows[r : r + 1] for r in range(rows.shape[0])], axis=1)


def taps_of(normed, weight_ref, sum_ref, rows):
    first = dot(normed, weight_ref[0])
    centre = dot(normed, weight_ref[1])
    third = dot(normed, weight_ref[2])
    sum_ref[...] = first[: rows + SUB] + third[SUB:]
    return centre[SUB : SUB + rows] + sum_ref[DILATION_ROWS : DILATION_ROWS + rows]


def stem_kernel(
    place_ref,
    codes_hbm,
    stem_weight_hbm,
    conv_gain_hbm,
    dilated_hbm,
    widen_hbm,
    token_gain_hbm,
    proj_hbm,
    stem_ref,
    normed_ref,
    taps_ref,
    edge_weight_ref,
    stem_weight_ref,
    conv_gain_ref,
    widen_ref,
    token_gain_ref,
    proj_ref,
    codes_ref,
    near_ref,
    dilated_ref,
    sum_ref,
    sems,
):
    copies = [
        pltpu.make_async_copy(source, target, sems.at[n])
        for n, (source, target) in enumerate(
            (
                (codes_hbm, codes_ref),
                (stem_weight_hbm, stem_weight_ref),
                (conv_gain_hbm, conv_gain_ref),
                (dilated_hbm, dilated_ref),
                (widen_hbm, widen_ref),
                (token_gain_hbm, token_gain_ref),
                (proj_hbm, proj_ref),
            )
        )
    ]
    for copy in copies:
        copy.start()
    core = place_ref[0]
    code_rows = codes_ref.shape[0] // 2
    rows = code_rows * SUB
    ext = rows + 2 * SUB
    for copy in copies[:3]:
        copy.wait()
    own = jnp.where(core == 0, codes_ref[:code_rows], codes_ref[code_rows:])
    near_ref[SUB : SUB + code_rows] = own
    near_ref[0:SUB] = codes_ref[code_rows - SUB : code_rows]
    near_ref[SUB + code_rows : 2 * SUB + code_rows] = codes_ref[code_rows : code_rows + SUB]
    tiles = [
        near_ref[pl.ds(SUB - 1 + r, SUB, stride=0), :] for r in range(code_rows + 2)
    ]
    row = iota((ext, 4 * PATCH), 0)
    valid = ((row >= SUB) | (core > 0)) & ((row < ext - SUB) | (core == 0))
    stem, normed = stem_of(
        spread_codes(tiles), valid, stem_weight_ref[...], in_lanes(conv_gain_ref[...])
    )
    stem_ref[...] = stem[SUB : SUB + rows].astype(jnp.bfloat16)
    normed_ref[...] = normed
    copies[3].wait()
    taps_ref[...] = taps_of(normed, dilated_ref, sum_ref, rows)
    edge_weight_ref[...] = dilated_ref[2 * core]
    for copy in copies[4:]:
        copy.wait()


def stem_call(place, codes, stem_weight, conv_gain, dilated, widen, token_gain, proj):
    channels = stem_weight.shape[1]
    half, wide = dilated.shape[2], widen.shape[1]
    rows = codes.shape[0] // 2 * SUB
    shape = jax.ShapeDtypeStruct
    out_shape = (
        shape((rows, channels), jnp.bfloat16),
        shape((rows + 2 * SUB, channels), jnp.bfloat16),
        shape((rows, half), jnp.float32),
        shape((channels, half), jnp.bfloat16),
        shape(stem_weight.shape, jnp.bfloat16),
        shape(conv_gain.shape, jnp.float32),
        shape(widen.shape, jnp.bfloat16),
        shape(token_gain.shape, jnp.float32),
        shape(proj.shape, jnp.bfloat16),
    )
    return pl.pallas_call(
        stem_kernel,
        out_shape=out_shape,
        in_specs=[SMEM] + [HBM] * 7,
        out_specs=(VMEM,) * len(out_shape),
        scratch_shapes=[
            pltpu.VMEM(codes.shape, jnp.int32),
            pltpu.VMEM((codes.shape[0] // 2 + 3 * SUB, LANES), jnp.int32),
            pltpu.VMEM(dilated.shape, jnp.bfloat16),
            pltpu.VMEM((rows + SUB, half), jnp.float32),
            pltpu.SemaphoreType.DMA((7,)),
        ],
        compiler_params=pltpu.CompilerParams(vmem_limit_bytes=LIMIT),
        cost_estimate=pl.CostEstimate(
            flops=6 * rows * channels * half, bytes_accessed=4 << 20, transcendentals=0
        ),
        name="stem",
    )(place, codes, stem_weight, conv_gain, dilated, widen, token_gain, proj)


def tower_kernel(
    place_ref,
    received_ref,
    stem_ref,
    normed_ref,
    taps_ref,
    edge_weight_ref,
    stem_weight_ref,
    conv_gain_ref,
    dilated_ref,
    halved_ref,
    near_ref,
    sum_ref,
    tower_ref,
):
    core, outside = place_ref[0], place_ref[1]
    rows = stem_ref.shape[0]
    half = taps_ref.shape[1]
    end = received_ref.shape[0]
    near_ref[0:SUB] = jnp.where(core == 0, received_ref[end - SUB :], received_ref[:SUB])
    near_ref[SUB:] = jnp.zeros((SUB, LANES), jnp.int32)
    tile = jnp.where(
        core == 0,
        near_ref[pl.ds(SUB - 1, SUB, stride=0), :],
        near_ref[pl.ds(0, SUB, stride=0), :],
    )
    _, edge = stem_of(
        spread_codes([tile]), outside > 0, stem_weight_ref[...], in_lanes(conv_gain_ref[...])
    )
    other_taps = taps_of(normed_ref[...], dilated_ref, sum_ref, rows)
    for taps, edge_weight, which in (
        (taps_ref[...], edge_weight_ref[...], core),
        (other_taps, dilated_ref[2 * core], 1 - core),
    ):
        added = pltpu.roll(dot(edge, edge_weight), DILATION_ROWS, 0)
        row = iota(added.shape, 0)
        head = jnp.where((row < DILATION_ROWS) & (core == 0), added, 0.0)
        tail = jnp.where((row >= DILATION_ROWS) & (core > 0), added, 0.0)
        taps = jnp.concatenate(
            [taps[:SUB] + head, taps[SUB : rows - SUB], taps[rows - SUB :] + tail], axis=0
        )
        columns = pl.ds(pl.multiple_of(which * half, LANES), half)
        tower = stem_ref[:, columns].astype(jnp.float32) + jax.nn.gelu(taps)
        pooled = []
        for c in range(half // LANES):
            tower_ref[c] = tower[:, c * LANES : (c + 1) * LANES]
            even = tower_ref[c, pl.ds(0, rows // 2, stride=2), :]
            odd = tower_ref[c, pl.ds(1, rows // 2, stride=2), :]
            pooled.append(jnp.maximum(even, odd))
        halved_ref[:, columns] = jnp.concatenate(pooled, axis=1).astype(jnp.bfloat16)


def tower_call(place, received, stem, normed, taps, edge_weight, stem_weight, conv_gain, dilated):
    rows, channels = stem.shape
    half = taps.shape[1]
    return pl.pallas_call(
        tower_kernel,
        out_shape=jax.ShapeDtypeStruct((rows // 2, channels), jnp.bfloat16),
        in_specs=[SMEM] + [VMEM] * 8,
        out_specs=VMEM,
        scratch_shapes=[
            pltpu.VMEM((2 * SUB, LANES), jnp.int32),
            pltpu.VMEM((rows + SUB, half), jnp.float32),
            pltpu.VMEM((half // LANES, rows, LANES), jnp.float32),
        ],
        compiler_params=pltpu.CompilerParams(vmem_limit_bytes=LIMIT),
        cost_estimate=pl.CostEstimate(
            flops=6 * rows * channels * half,
            bytes_accessed=4 << 20,
            transcendentals=rows * channels,
        ),
        name="tower",
    )(place, received, stem, normed, taps, edge_weight, stem_weight, conv_gain, dilated)


def widen_kernel(
    place_ref,
    halved_ref,
    widen_ref,
    widen_other_ref,
    token_gain_ref,
    proj_ref,
    fine_ref,
    fine_other_ref,
    spread_ref,
):
    core = place_ref[0]
    halved = halved_ref[...]
    token_count = halved.shape[0] // POOL
    tokens = []
    for weight_ref, out_ref in ((widen_ref, fine_ref), (widen_other_ref, fine_other_ref)):
        fine = jax.nn.gelu(dot(halved, weight_ref[...])).astype(jnp.bfloat16)
        out_ref[...] = fine
        fine = fine.astype(jnp.float32)
        tokens.append(
            jnp.concatenate(
                [
                    jnp.mean(fine[t * POOL : (t + 1) * POOL], axis=0, keepdims=True)
                    for t in range(token_count)
                ],
                axis=0,
            )
            .astype(jnp.bfloat16)
            .astype(jnp.float32)
        )
    wide = widen_ref.shape[1]
    squares = sum(jnp.sum(t * t, axis=1, keepdims=True) for t in tokens)
    scale = lax.rsqrt(squares / (2 * wide) + epsilon)
    gain = token_gain_ref[...]
    gain_rows = wide // LANES
    gains = [in_lanes(gain[:gain_rows]), in_lanes(gain[gain_rows:])]
    factors = 0.0
    for token, which in zip(tokens, (core, 1 - core)):
        start = pl.multiple_of(which * wide, LANES)
        gain = jnp.where(which == 0, gains[0], gains[1])
        factors = factors + dot(
            (token * scale * gain).astype(jnp.bfloat16), proj_ref[pl.ds(start, wide), :]
        )
    spread_ref[...] = jnp.broadcast_to(factors.astype(jnp.bfloat16)[None], spread_ref.shape)


def widen_call(place, halved, widen, widen_other, token_gain, proj, members):
    rows, channels = halved.shape
    wide = widen.shape[1]
    fine = jax.ShapeDtypeStruct((rows, wide), jnp.bfloat16)
    spread = jax.ShapeDtypeStruct((members, rows // POOL, 2 * PC), jnp.bfloat16)
    return pl.pallas_call(
        widen_kernel,
        out_shape=(fine, fine, spread),
        in_specs=[SMEM] + [VMEM] * 5,
        out_specs=(VMEM,) * 3,
        compiler_params=pltpu.CompilerParams(vmem_limit_bytes=LIMIT),
        cost_estimate=pl.CostEstimate(
            flops=4 * rows * channels * wide,
            bytes_accessed=4 << 20,
            transcendentals=2 * rows * wide,
        ),
        name="widen",
    )(place, halved, widen, widen_other, token_gain, proj)


def arrange_kernel(place_ref, one_ref, other_ref, two_ref, _, out_one_ref, out_two_ref):
    core = place_ref[0]
    part = one_ref.shape[2]
    for a in range(3):
        for b in range(3):
            columns = slice(b * PC, (b + 1) * PC)
            for ref, which in ((one_ref, core), (other_ref, 1 - core)):
                start = pl.multiple_of(a * PC + which * part, part)
                out_one_ref[pl.ds(start, part), columns] = ref[a, b]
            two = two_ref[a, b]
            out_two_ref[a * PC : a * PC + part, columns] = two
            out_two_ref[a * PC + part : (a + 1) * PC, columns] = two


def arrange_call(place, one, other, two, after):
    out = jax.ShapeDtypeStruct((3 * PC, 3 * PC), jnp.bfloat16)
    return pl.pallas_call(
        arrange_kernel,
        out_shape=(out, out),
        in_specs=[SMEM] + [VMEM] * 3 + [ANY],
        out_specs=(VMEM, VMEM),
        compiler_params=pltpu.CompilerParams(vmem_limit_bytes=LIMIT),
        cost_estimate=pl.CostEstimate(flops=0, bytes_accessed=2 << 20, transcendentals=0),
        name="arrange",
    )(place, one, other, two, after)


def pair_kernel(
    tokens_total,
    height,
    width,
    place_ref,
    every_ref,
    dist_ref,
    weight_one_ref,
    weight_two_ref,
    fine_ref,
    fine_received_ref,
    fine_hbm,
    out_hbm,
    row_ref,
    col_ref,
    out_ref,
    sems,
):
    core, row_anchor, col_anchor = place_ref[0], place_ref[2], place_ref[3]
    fine_rows = fine_ref.shape[0]
    copies = []
    for n, (source, which) in enumerate(((fine_ref, core), (fine_received_ref, 1 - core))):
        start = pl.multiple_of(which * fine_rows, fine_rows)
        copies.append(
            pltpu.make_async_copy(source, fine_hbm.at[pl.ds(start, fine_rows)], sems.at[n])
        )
    for copy in copies:
        copy.start()
    members, per = every_ref.shape[0], every_ref.shape[1]
    cols = width + SUB
    high = height + 4
    for ref in (row_ref, col_ref):
        ref[0:SUB] = jnp.zeros((SUB, PC), jnp.float32)
        ref[tokens_total : tokens_total + 2 * SUB] = jnp.zeros((2 * SUB, PC), jnp.float32)
    for m in range(members):
        factors = every_ref[m].astype(jnp.float32)
        row_ref[2 + m * per : 2 + (m + 1) * per] = factors[:, :PC]
        col_ref[2 + m * per : 2 + (m + 1) * per] = factors[:, PC:]
    col_factor = col_ref[pl.ds(pl.multiple_of(col_anchor, SUB), cols), :]
    j = col_anchor - 2 + iota((cols, PC), 0)
    starts, masks = [], []
    for r in range(high):
        i = row_anchor - 2 + r
        row_factor = row_ref[pl.ds(row_anchor + r, SUB, stride=0), :]
        row_factor = jnp.concatenate([row_factor] * (cols // SUB), axis=0)
        distance = jnp.log1p(jnp.abs(i - j).astype(jnp.float32)) * (1.0 / math.log(tokens_total))
        starts.append(row_factor * col_factor + distance * dist_ref[...])
        masks.append(
            jnp.where((i >= 0) & (i < tokens_total) & (j >= 0) & (j < tokens_total), 1.0, 0.0)
        )
    start = jnp.concatenate(starts, axis=0).astype(jnp.bfloat16).astype(jnp.float32)
    mask = jnp.concatenate(masks, axis=0)

    def conv(active, weight):
        size = active.shape[0]
        shifted = [active] + [pltpu.roll(active, size - b, 0) for b in (1, 2)]
        wide = jnp.concatenate([s.astype(jnp.bfloat16) for s in shifted], axis=1)
        taps = lax.dot_general(
            wide, weight, (((1,), (1,)), ((), ())), preferred_element_type=jnp.float32
        )
        keep = size - 2 * cols
        return sum(taps[a * cols : a * cols + keep, a * PC : (a + 1) * PC] for a in range(3))

    size = high * cols
    centre = pltpu.roll(start, size - 1, 0)[cols : size - cols]
    centre_mask = pltpu.roll(mask, size - 1, 0)[cols : size - cols]
    mid = centre + conv(jax.nn.gelu(start) * mask, weight_one_ref[...])
    mid = mid.astype(jnp.bfloat16).astype(jnp.float32)
    result = conv(jax.nn.gelu(mid) * centre_mask, weight_two_ref[...])
    mid_size = mid.shape[0]
    mid_centre = pltpu.roll(mid, mid_size - 1, 0)[cols : mid_size - cols]
    own = pltpu.roll(mid_centre, core * (PC // 2), 1)
    result = result + own
    channels = out_ref.shape[2]
    for r in range(height):
        out_ref[r] = result[r * cols : r * cols + width, :channels].astype(jnp.bfloat16)
    copies.append(pltpu.make_async_copy(out_ref, out_hbm, sems.at[2]))
    copies[2].start()
    for copy in copies:
        copy.wait()


def pair_call(
    place,
    every,
    dist_weight,
    weight_one,
    weight_two,
    fine,
    fine_received,
    tokens_total,
    height,
    width,
):
    channels = PC // 2
    rows, wide = fine.shape
    return pl.pallas_call(
        functools.partial(pair_kernel, tokens_total, height, width),
        out_shape=(
            jax.ShapeDtypeStruct((2 * rows, wide), jnp.bfloat16),
            jax.ShapeDtypeStruct((height, width, channels), jnp.bfloat16),
        ),
        in_specs=[SMEM] + [VMEM] * 6,
        out_specs=(HBM, HBM),
        scratch_shapes=[
            pltpu.VMEM((tokens_total + 2 * SUB, PC), jnp.float32),
            pltpu.VMEM((tokens_total + 2 * SUB, PC), jnp.float32),
            pltpu.VMEM((height, width, channels), jnp.bfloat16),
            pltpu.SemaphoreType.DMA((3,)),
        ],
        compiler_params=pltpu.CompilerParams(vmem_limit_bytes=32 << 20),
        name="pair",
    )(place, every, dist_weight, weight_one, weight_two, fine, fine_received)


def per_device(
    base_codes,
    stem_weight,
    conv_gain,
    dilated_conv_weight,
    widen_weight,
    token_gain,
    proj_weight,
    dist_weight,
    pair_weight_one,
    pair_weight_two,
):
    seq_count = lax.axis_size("seq")
    section_count = lax.axis_size("section")
    core_count = lax.axis_size("chan")
    chip_count = seq_count * section_count
    members = chip_count * core_count
    core = lax.axis_index("chan")
    chip = lax.axis_index(CHIPS)
    last = core_count - 1

    codes = base_codes.reshape(-1, LANES)
    pairs = []
    for i in range(chip_count - 1):
        low, high = i * core_count + last, (i + 1) * core_count
        pairs += [(low, high), (high, low)]
    received = lax.ppermute(codes, PART, pairs)
    dilated_other = swap(dilated_conv_weight)
    widen_other = swap(widen_weight)
    pair_one = pair_weight_one.swapaxes(2, 3)
    pair_two = pair_weight_two.swapaxes(2, 3)
    pair_one_other = swap(pair_one)

    tokens_total = codes.shape[0] * LANES // PATCH // 2 // POOL * chip_count
    height = tokens_total // seq_count
    width = tokens_total // section_count
    place = jnp.stack(
        [
            core,
            jnp.where(core == 0, chip > 0, chip < chip_count - 1).astype(jnp.int32),
            lax.axis_index("seq") * height,
            lax.axis_index("section") * width,
        ]
    )
    gain_rows = conv_gain.reshape(-1, LANES)
    token_gain_rows = token_gain.reshape(-1, LANES)
    in_hbm = functools.partial(pltpu.with_memory_space_constraint, memory_space=pltpu.HBM)
    stem, normed, taps, edge_weight, stem_weight, gain_rows, widen_own, token_gain_rows, proj = (
        stem_call(
            place,
            in_hbm(codes),
            in_hbm(stem_weight),
            in_hbm(gain_rows),
            in_hbm(dilated_conv_weight),
            in_hbm(widen_weight),
            in_hbm(token_gain_rows),
            in_hbm(proj_weight),
        )
    )
    halved = tower_call(
        place, received, stem, normed, taps, edge_weight, stem_weight, gain_rows, dilated_other
    )
    fine_own, fine_other, spread = widen_call(
        place, halved, widen_own, widen_other, token_gain_rows, proj, members
    )
    every = lax.all_to_all(spread, PART, 0, 0, tiled=True)
    fine_received = swap(fine_other)
    weight_one, weight_two = arrange_call(
        place, pair_one, pair_one_other, pair_two, fine_own
    )
    fine_features, pair_map = pair_call(
        place,
        every,
        dist_weight[None],
        weight_one,
        weight_two,
        fine_own,
        fine_received,
        tokens_total,
        height,
        width,
    )
    return (fine_features, pair_map.transpose(2, 0, 1))


def solution(mesh):
    in_specs = (
        P(("groups", "seq", "section")),
        P(),
        P(),
        P(None, None, "chan"),
        P(None, "chan"),
        P(),
        P(),
        P(),
        P(None, None, None, "chan"),
        P(None, None, None, "chan"),
    )
    out_specs = (P(("groups", "seq", "section"), "chan"), P("chan", ("groups", "seq"), "section"))
    return jax.shard_map(
        per_device, mesh=mesh, in_specs=in_specs, out_specs=out_specs, check_vma=False
    )
```

```python
import functools
import math

import jax
import jax.numpy as jnp
from jax import lax
from jax.experimental import pallas as pl
from jax.experimental.pallas import tpu as pltpu
from jax.sharding import PartitionSpec as P


PC = 128
PATCH = 16
POOL = 64
DILATION_ROWS = 4


epsilon = 1e-06
LANES = 128
SUB = 8
CHIPS = ("seq", "section")
ALL = ("groups", "seq", "section", "chan")
VMEM = pl.BlockSpec(memory_space=pltpu.VMEM)
SMEM = pl.BlockSpec(memory_space=pltpu.SMEM)
HBM = pl.BlockSpec(memory_space=pltpu.HBM)
ANY = pl.BlockSpec(memory_space=pl.ANY)
LIMIT = 16 << 20


def swap(values):
    count = lax.axis_size("chan")
    return lax.ppermute(values, "chan", [(i, count - 1 - i) for i in range(count)])


def dot(a, b):
    return jnp.dot(a, b, preferred_element_type=jnp.float32)


def iota(shape, axis):
    return lax.broadcasted_iota(jnp.int32, shape, axis)


def spread_codes(tiles):
    own_patch = iota((SUB, LANES), 1) // PATCH == iota((SUB, LANES), 0)
    picked = jnp.concatenate(
        [jnp.where(own_patch, t, 0).astype(jnp.float32) for t in tiles], axis=0
    ).astype(jnp.bfloat16)
    width = 4 * PATCH
    gather = (iota((LANES, width), 0) % PATCH == iota((LANES, width), 1) // 4).astype(jnp.bfloat16)
    return dot(picked, gather)


def stem_of(codes, valid, stem_weight, gain):
    base = (iota(codes.shape, 1) % 4).astype(jnp.float32)
    onehot = jnp.where((codes == base) & valid, 1.0, 0.0).astype(jnp.bfloat16)
    stem = dot(onehot, stem_weight).astype(jnp.bfloat16).astype(jnp.float32)
    mean_square = jnp.mean(stem * stem, axis=1, keepdims=True)
    normed = (stem * lax.rsqrt(mean_square + epsilon) * gain).astype(jnp.bfloat16)
    return stem, normed


def in_lanes(rows):
    return jnp.concatenate([rows[r : r + 1] for r in range(rows.shape[0])], axis=1)


def taps_of(normed, weight_ref, sum_ref, rows):
    first = dot(normed, weight_ref[0])
    centre = dot(normed, weight_ref[1])
    third = dot(normed, weight_ref[2])
    sum_ref[...] = first[: rows + SUB] + third[SUB:]
    return centre[SUB : SUB + rows] + sum_ref[DILATION_ROWS : DILATION_ROWS + rows]


def stem_kernel(
    place_ref,
    codes_hbm,
    stem_weight_hbm,
    conv_gain_hbm,
    dilated_hbm,
    widen_hbm,
    token_gain_hbm,
    proj_hbm,
    stem_ref,
    normed_ref,
    taps_ref,
    edge_weight_ref,
    stem_weight_ref,
    conv_gain_ref,
    widen_ref,
    token_gain_ref,
    proj_ref,
    codes_ref,
    near_ref,
    dilated_ref,
    sum_ref,
    sems,
):
    copies = [
        pltpu.make_async_copy(source, target, sems.at[n])
        for n, (source, target) in enumerate(
            (
                (codes_hbm, codes_ref),
                (stem_weight_hbm, stem_weight_ref),
                (conv_gain_hbm, conv_gain_ref),
                (dilated_hbm, dilated_ref),
                (widen_hbm, widen_ref),
                (token_gain_hbm, token_gain_ref),
                (proj_hbm, proj_ref),
            )
        )
    ]
    for copy in copies:
        copy.start()
    core = place_ref[0]
    code_rows = codes_ref.shape[0] // 2
    rows = code_rows * SUB
    ext = rows + 2 * SUB
    for copy in copies[:3]:
        copy.wait()
    own = jnp.where(core == 0, codes_ref[:code_rows], codes_ref[code_rows:])
    near_ref[SUB : SUB + code_rows] = own
    near_ref[0:SUB] = codes_ref[code_rows - SUB : code_rows]
    near_ref[SUB + code_rows : 2 * SUB + code_rows] = codes_ref[code_rows : code_rows + SUB]
    tiles = [
        near_ref[pl.ds(SUB - 1 + r, SUB, stride=0), :] for r in range(code_rows + 2)
    ]
    row = iota((ext, 4 * PATCH), 0)
    valid = ((row >= SUB) | (core > 0)) & ((row < ext - SUB) | (core == 0))
    stem, normed = stem_of(
        spread_codes(tiles), valid, stem_weight_ref[...], in_lanes(conv_gain_ref[...])
    )
    stem_ref[...] = stem[SUB : SUB + rows].astype(jnp.bfloat16)
    normed_ref[...] = normed
    copies[3].wait()
    taps_ref[...] = taps_of(normed, dilated_ref, sum_ref, rows)
    edge_weight_ref[...] = dilated_ref[2 * core]
    for copy in copies[4:]:
        copy.wait()


def stem_call(place, codes, stem_weight, conv_gain, dilated, widen, token_gain, proj):
    channels = stem_weight.shape[1]
    half = dilated.shape[2]
    rows = codes.shape[0] // 2 * SUB
    shape = jax.ShapeDtypeStruct
    out_shape = (
        shape((rows, channels), jnp.bfloat16),
        shape((rows + 2 * SUB, channels), jnp.bfloat16),
        shape((rows, half), jnp.float32),
        shape((channels, half), jnp.bfloat16),
        shape(stem_weight.shape, jnp.bfloat16),
        shape(conv_gain.shape, jnp.float32),
        shape(widen.shape, jnp.bfloat16),
        shape(token_gain.shape, jnp.float32),
        shape(proj.shape, jnp.bfloat16),
    )
    return pl.pallas_call(
        stem_kernel,
        out_shape=out_shape,
        in_specs=[SMEM] + [HBM] * 7,
        out_specs=(VMEM,) * len(out_shape),
        scratch_shapes=[
            pltpu.VMEM(codes.shape, jnp.int32),
            pltpu.VMEM((codes.shape[0] // 2 + 3 * SUB, LANES), jnp.int32),
            pltpu.VMEM(dilated.shape, jnp.bfloat16),
            pltpu.VMEM((rows + SUB, half), jnp.float32),
            pltpu.SemaphoreType.DMA((7,)),
        ],
        compiler_params=pltpu.CompilerParams(vmem_limit_bytes=LIMIT),
        cost_estimate=pl.CostEstimate(
            flops=6 * rows * channels * half, bytes_accessed=4 << 20, transcendentals=0
        ),
        name="stem",
    )(place, codes, stem_weight, conv_gain, dilated, widen, token_gain, proj)


def tower_kernel(
    place_ref,
    received_ref,
    stem_ref,
    normed_ref,
    taps_ref,
    edge_weight_ref,
    stem_weight_ref,
    conv_gain_ref,
    dilated_ref,
    halved_ref,
    near_ref,
    sum_ref,
    tower_ref,
):
    core, outside = place_ref[0], place_ref[1]
    rows = stem_ref.shape[0]
    half = taps_ref.shape[1]
    end = received_ref.shape[0]
    near_ref[0:SUB] = jnp.where(core == 0, received_ref[end - SUB :], received_ref[:SUB])
    near_ref[SUB:] = jnp.zeros((SUB, LANES), jnp.int32)
    tile = jnp.where(
        core == 0,
        near_ref[pl.ds(SUB - 1, SUB, stride=0), :],
        near_ref[pl.ds(0, SUB, stride=0), :],
    )
    _, edge = stem_of(
        spread_codes([tile]), outside > 0, stem_weight_ref[...], in_lanes(conv_gain_ref[...])
    )
    other_taps = taps_of(normed_ref[...], dilated_ref, sum_ref, rows)
    for taps, edge_weight, which in (
        (taps_ref[...], edge_weight_ref[...], core),
        (other_taps, dilated_ref[2 * core], 1 - core),
    ):
        added = pltpu.roll(dot(edge, edge_weight), DILATION_ROWS, 0)
        row = iota(added.shape, 0)
        head = jnp.where((row < DILATION_ROWS) & (core == 0), added, 0.0)
        tail = jnp.where((row >= DILATION_ROWS) & (core > 0), added, 0.0)
        taps = jnp.concatenate(
            [taps[:SUB] + head, taps[SUB : rows - SUB], taps[rows - SUB :] + tail], axis=0
        )
        columns = pl.ds(pl.multiple_of(which * half, LANES), half)
        tower = stem_ref[:, columns].astype(jnp.float32) + jax.nn.gelu(taps)
        pooled = []
        for c in range(half // LANES):
            tower_ref[c] = tower[:, c * LANES : (c + 1) * LANES]
            even = tower_ref[c, pl.ds(0, rows // 2, stride=2), :]
            odd = tower_ref[c, pl.ds(1, rows // 2, stride=2), :]
            pooled.append(jnp.maximum(even, odd))
        halved_ref[:, columns] = jnp.concatenate(pooled, axis=1).astype(jnp.bfloat16)


def tower_call(place, received, stem, normed, taps, edge_weight, stem_weight, conv_gain, dilated):
    rows, channels = stem.shape
    half = taps.shape[1]
    return pl.pallas_call(
        tower_kernel,
        out_shape=jax.ShapeDtypeStruct((rows // 2, channels), jnp.bfloat16),
        in_specs=[SMEM] + [VMEM] * 8,
        out_specs=VMEM,
        scratch_shapes=[
            pltpu.VMEM((2 * SUB, LANES), jnp.int32),
            pltpu.VMEM((rows + SUB, half), jnp.float32),
            pltpu.VMEM((half // LANES, rows, LANES), jnp.float32),
        ],
        compiler_params=pltpu.CompilerParams(vmem_limit_bytes=LIMIT),
        cost_estimate=pl.CostEstimate(
            flops=6 * rows * channels * half,
            bytes_accessed=4 << 20,
            transcendentals=rows * channels,
        ),
        name="tower",
    )(place, received, stem, normed, taps, edge_weight, stem_weight, conv_gain, dilated)


def widen_kernel(
    place_ref,
    halved_ref,
    widen_ref,
    widen_other_ref,
    token_gain_ref,
    proj_ref,
    fine_ref,
    fine_other_ref,
    spread_ref,
):
    core = place_ref[0]
    halved = halved_ref[...]
    token_count = halved.shape[0] // POOL
    tokens = []
    for weight_ref, out_ref in ((widen_ref, fine_ref), (widen_other_ref, fine_other_ref)):
        fine = jax.nn.gelu(dot(halved, weight_ref[...])).astype(jnp.bfloat16)
        out_ref[...] = fine
        fine = fine.astype(jnp.float32)
        tokens.append(
            jnp.concatenate(
                [
                    jnp.mean(fine[t * POOL : (t + 1) * POOL], axis=0, keepdims=True)
                    for t in range(token_count)
                ],
                axis=0,
            )
            .astype(jnp.bfloat16)
            .astype(jnp.float32)
        )
    wide = widen_ref.shape[1]
    squares = sum(jnp.sum(t * t, axis=1, keepdims=True) for t in tokens)
    scale = lax.rsqrt(squares / (2 * wide) + epsilon)
    gain = token_gain_ref[...]
    gain_rows = wide // LANES
    gains = [in_lanes(gain[:gain_rows]), in_lanes(gain[gain_rows:])]
    factors = 0.0
    for token, which in zip(tokens, (core, 1 - core)):
        start = pl.multiple_of(which * wide, LANES)
        gain = jnp.where(which == 0, gains[0], gains[1])
        factors = factors + dot(
            (token * scale * gain).astype(jnp.bfloat16), proj_ref[pl.ds(start, wide), :]
        )
    spread_ref[...] = jnp.broadcast_to(factors.astype(jnp.bfloat16)[None], spread_ref.shape)


def widen_call(place, halved, widen, widen_other, token_gain, proj, members):
    rows, channels = halved.shape
    wide = widen.shape[1]
    fine = jax.ShapeDtypeStruct((rows, wide), jnp.bfloat16)
    spread = jax.ShapeDtypeStruct((members, rows // POOL, 2 * PC), jnp.bfloat16)
    return pl.pallas_call(
        widen_kernel,
        out_shape=(fine, fine, spread),
        in_specs=[SMEM] + [VMEM] * 5,
        out_specs=(VMEM,) * 3,
        compiler_params=pltpu.CompilerParams(vmem_limit_bytes=LIMIT),
        cost_estimate=pl.CostEstimate(
            flops=4 * rows * channels * wide,
            bytes_accessed=4 << 20,
            transcendentals=2 * rows * wide,
        ),
        name="widen",
    )(place, halved, widen, widen_other, token_gain, proj)


def arrange_kernel(place_ref, one_ref, other_ref, two_ref, _, out_one_ref, out_two_ref):
    core = place_ref[0]
    part = one_ref.shape[2]
    for a in range(3):
        for b in range(3):
            columns = slice(b * PC, (b + 1) * PC)
            for ref, which in ((one_ref, core), (other_ref, 1 - core)):
                start = pl.multiple_of(a * PC + which * part, part)
                out_one_ref[pl.ds(start, part), columns] = ref[a, b]
            two = two_ref[a, b]
            out_two_ref[a * PC : a * PC + part, columns] = two
            out_two_ref[a * PC + part : (a + 1) * PC, columns] = two


def arrange_call(place, one, other, two, after):
    out = jax.ShapeDtypeStruct((3 * PC, 3 * PC), jnp.bfloat16)
    return pl.pallas_call(
        arrange_kernel,
        out_shape=(out, out),
        in_specs=[SMEM] + [VMEM] * 3 + [ANY],
        out_specs=(VMEM, VMEM),
        compiler_params=pltpu.CompilerParams(vmem_limit_bytes=LIMIT),
        cost_estimate=pl.CostEstimate(flops=0, bytes_accessed=2 << 20, transcendentals=0),
        name="arrange",
    )(place, one, other, two, after)


def pair_kernel(
    tokens_total,
    height,
    width,
    place_ref,
    every_ref,
    dist_ref,
    weight_one_ref,
    weight_two_ref,
    fine_ref,
    fine_received_ref,
    fine_hbm,
    out_hbm,
    row_ref,
    col_ref,
    out_ref,
    sems,
):
    core, row_anchor, col_anchor = place_ref[0], place_ref[2], place_ref[3]
    fine_rows = fine_ref.shape[0]
    copies = []
    for n, (source, which) in enumerate(((fine_ref, core), (fine_received_ref, 1 - core))):
        start = pl.multiple_of(which * fine_rows, fine_rows)
        copies.append(
            pltpu.make_async_copy(source, fine_hbm.at[pl.ds(start, fine_rows)], sems.at[n])
        )
    for copy in copies:
        copy.start()
    per = every_ref.shape[1]
    members = tokens_total // per
    group_start = place_ref[4]
    cols = width + SUB
    high = height + 4
    for ref in (row_ref, col_ref):
        ref[0:SUB] = jnp.zeros((SUB, PC), jnp.float32)
        ref[tokens_total : tokens_total + 2 * SUB] = jnp.zeros((2 * SUB, PC), jnp.float32)
    for m in range(members):
        factors = every_ref[group_start + m].astype(jnp.float32)
        row_ref[2 + m * per : 2 + (m + 1) * per] = factors[:, :PC]
        col_ref[2 + m * per : 2 + (m + 1) * per] = factors[:, PC:]
    col_factor = col_ref[pl.ds(pl.multiple_of(col_anchor, SUB), cols), :]
    j = col_anchor - 2 + iota((cols, PC), 0)
    starts, masks = [], []
    for r in range(high):
        i = row_anchor - 2 + r
        row_factor = row_ref[pl.ds(row_anchor + r, SUB, stride=0), :]
        row_factor = jnp.concatenate([row_factor] * (cols // SUB), axis=0)
        distance = jnp.log1p(jnp.abs(i - j).astype(jnp.float32)) * (1.0 / math.log(tokens_total))
        starts.append(row_factor * col_factor + distance * dist_ref[...])
        masks.append(
            jnp.where((i >= 0) & (i < tokens_total) & (j >= 0) & (j < tokens_total), 1.0, 0.0)
        )
    start = jnp.concatenate(starts, axis=0).astype(jnp.bfloat16).astype(jnp.float32)
    mask = jnp.concatenate(masks, axis=0)

    def conv(active, weight):
        size = active.shape[0]
        shifted = [active] + [pltpu.roll(active, size - b, 0) for b in (1, 2)]
        wide = jnp.concatenate([s.astype(jnp.bfloat16) for s in shifted], axis=1)
        taps = lax.dot_general(
            wide, weight, (((1,), (1,)), ((), ())), preferred_element_type=jnp.float32
        )
        keep = size - 2 * cols
        return sum(taps[a * cols : a * cols + keep, a * PC : (a + 1) * PC] for a in range(3))

    size = high * cols
    centre = pltpu.roll(start, size - 1, 0)[cols : size - cols]
    centre_mask = pltpu.roll(mask, size - 1, 0)[cols : size - cols]
    mid = centre + conv(jax.nn.gelu(start) * mask, weight_one_ref[...])
    mid = mid.astype(jnp.bfloat16).astype(jnp.float32)
    result = conv(jax.nn.gelu(mid) * centre_mask, weight_two_ref[...])
    mid_size = mid.shape[0]
    mid_centre = pltpu.roll(mid, mid_size - 1, 0)[cols : mid_size - cols]
    own = pltpu.roll(mid_centre, core * (PC // 2), 1)
    result = result + own
    channels = out_ref.shape[2]
    for r in range(height):
        out_ref[r] = result[r * cols : r * cols + width, :channels].astype(jnp.bfloat16)
    copies.append(pltpu.make_async_copy(out_ref, out_hbm, sems.at[2]))
    copies[2].start()
    for copy in copies:
        copy.wait()


def pair_call(
    place,
    every,
    dist_weight,
    weight_one,
    weight_two,
    fine,
    fine_received,
    tokens_total,
    height,
    width,
):
    channels = PC // 2
    rows, wide = fine.shape
    return pl.pallas_call(
        functools.partial(pair_kernel, tokens_total, height, width),
        out_shape=(
            jax.ShapeDtypeStruct((2 * rows, wide), jnp.bfloat16),
            jax.ShapeDtypeStruct((height, width, channels), jnp.bfloat16),
        ),
        in_specs=[SMEM] + [VMEM] * 6,
        out_specs=(HBM, HBM),
        scratch_shapes=[
            pltpu.VMEM((tokens_total + 2 * SUB, PC), jnp.float32),
            pltpu.VMEM((tokens_total + 2 * SUB, PC), jnp.float32),
            pltpu.VMEM((height, width, channels), jnp.bfloat16),
            pltpu.SemaphoreType.DMA((3,)),
        ],
        compiler_params=pltpu.CompilerParams(vmem_limit_bytes=32 << 20),
        name="pair",
    )(place, every, dist_weight, weight_one, weight_two, fine, fine_received)


def per_device(
    base_codes,
    stem_weight,
    conv_gain,
    dilated_conv_weight,
    widen_weight,
    token_gain,
    proj_weight,
    dist_weight,
    pair_weight_one,
    pair_weight_two,
):
    seq_count = lax.axis_size("seq")
    section_count = lax.axis_size("section")
    core_count = lax.axis_size("chan")
    chip_count = seq_count * section_count
    members = chip_count * core_count
    group_count = lax.axis_size("groups")
    core = lax.axis_index("chan")
    chip = lax.axis_index(CHIPS)
    last = core_count - 1

    codes = base_codes.reshape(-1, LANES)
    pairs = []
    for g in range(group_count):
        device = [(g * chip_count + i) * core_count for i in range(chip_count)]
        for low, high in zip(device[:-1], device[1:]):
            pairs += [(low + last, high), (high, low + last)]
        following = (g + 1) % group_count * members
        pairs += [(device[0], following), (device[-1] + last, following + members - 1)]
    received = lax.ppermute(codes, ALL, pairs)
    dilated_other = swap(dilated_conv_weight)
    widen_other = swap(widen_weight)
    pair_one = pair_weight_one.swapaxes(2, 3)
    pair_two = pair_weight_two.swapaxes(2, 3)
    pair_one_other = swap(pair_one)

    tokens_total = codes.shape[0] * LANES // PATCH // 2 // POOL * chip_count
    height = tokens_total // seq_count
    width = tokens_total // section_count
    place = jnp.stack(
        [
            core,
            jnp.where(core == 0, chip > 0, chip < chip_count - 1).astype(jnp.int32),
            lax.axis_index("seq") * height,
            lax.axis_index("section") * width,
            lax.axis_index("groups") * members,
        ]
    )
    gain_rows = conv_gain.reshape(-1, LANES)
    token_gain_rows = token_gain.reshape(-1, LANES)
    in_hbm = functools.partial(pltpu.with_memory_space_constraint, memory_space=pltpu.HBM)
    stem, normed, taps, edge_weight, stem_weight, gain_rows, widen_own, token_gain_rows, proj = (
        stem_call(
            place,
            in_hbm(codes),
            in_hbm(stem_weight),
            in_hbm(gain_rows),
            in_hbm(dilated_conv_weight),
            in_hbm(widen_weight),
            in_hbm(token_gain_rows),
            in_hbm(proj_weight),
        )
    )
    halved = tower_call(
        place, received, stem, normed, taps, edge_weight, stem_weight, gain_rows, dilated_other
    )
    fine_own, fine_other, spread = widen_call(
        place, halved, widen_own, widen_other, token_gain_rows, proj, group_count * members
    )
    every = lax.all_to_all(spread, ALL, 0, 0, tiled=True)
    fine_received = swap(fine_other)
    weight_one, weight_two = arrange_call(
        place, pair_one, pair_one_other, pair_two, fine_own
    )
    fine_features, pair_map = pair_call(
        place,
        every,
        dist_weight[None],
        weight_one,
        weight_two,
        fine_own,
        fine_received,
        tokens_total,
        height,
        width,
    )
    return (fine_features, pair_map.transpose(2, 0, 1))


def solution(mesh):
    in_specs = (
        P(("groups", "seq", "section")),
        P(),
        P(),
        P(None, None, "chan"),
        P(None, "chan"),
        P(),
        P(),
        P(),
        P(None, None, None, "chan"),
        P(None, None, None, "chan"),
    )
    out_specs = (P(("groups", "seq", "section"), "chan"), P("chan", ("groups", "seq"), "section"))

    return jax.shard_map(
        per_device, mesh=mesh, in_specs=in_specs, out_specs=out_specs, check_vma=False
    )
```

```python
import functools
import math

import jax
import jax.numpy as jnp
from jax import lax
from jax.experimental import pallas as pl
from jax.experimental.pallas import tpu as pltpu
from jax.sharding import PartitionSpec as P


PC = 128
PATCH = 16
POOL = 64
DILATION_ROWS = 4


epsilon = 1e-06
LANES = 128
SUB = 8
CHIPS = ("seq", "section")
ALL = ("groups", "seq", "section", "chan")
VMEM = pl.BlockSpec(memory_space=pltpu.VMEM)
SMEM = pl.BlockSpec(memory_space=pltpu.SMEM)
HBM = pl.BlockSpec(memory_space=pltpu.HBM)
ANY = pl.BlockSpec(memory_space=pl.ANY)
LIMIT = 16 << 20


def swap(values):
    count = lax.axis_size("chan")
    return lax.ppermute(values, "chan", [(i, count - 1 - i) for i in range(count)])


def dot(a, b):
    return jnp.dot(a, b, preferred_element_type=jnp.float32)


def gelu_of(part, share):
    linear = math.sqrt(2 / math.pi) / share
    cubic = 0.044715 * math.sqrt(2 / math.pi) / share**3
    return part + part * jnp.tanh(part * (linear + cubic * (part * part)))


def gelu(x):
    return gelu_of(0.5 * x, 0.5)


def iota(shape, axis):
    return lax.broadcasted_iota(jnp.int32, shape, axis)


def spread_codes(tiles):
    own_patch = iota((SUB, LANES), 1) // PATCH == iota((SUB, LANES), 0)
    picked = jnp.concatenate(
        [jnp.where(own_patch, t, 0).astype(jnp.float32) for t in tiles], axis=0
    ).astype(jnp.bfloat16)
    width = 4 * PATCH
    gather = (iota((LANES, width), 0) % PATCH == iota((LANES, width), 1) // 4).astype(jnp.bfloat16)
    return dot(picked, gather)


def stem_of(codes, valid, stem_weight, gain):
    base = (iota(codes.shape, 1) % 4).astype(jnp.float32)
    onehot = jnp.where((codes == base) & valid, 0.5, 0.0).astype(jnp.bfloat16)
    stem = dot(onehot, stem_weight)
    mean_square = jnp.mean(stem * stem, axis=1, keepdims=True)
    scale = 0.25 * lax.rsqrt(mean_square + 0.25 * epsilon)
    return stem, (stem * scale * gain).astype(jnp.bfloat16)


def in_lanes(rows):
    return jnp.concatenate([rows[r : r + 1] for r in range(rows.shape[0])], axis=1)


def taps_of(normed, weight_ref, sum_ref, rows, columns):
    first = dot(normed, weight_ref[0, :, columns])
    third = dot(normed, weight_ref[2, :, columns])
    centre = dot(normed, weight_ref[1, :, columns])
    sum_ref[:, columns] = first[: rows + SUB] + third[SUB:]
    return centre[SUB : SUB + rows] + sum_ref[DILATION_ROWS : DILATION_ROWS + rows, columns]


def stem_kernel(
    place_ref,
    codes_hbm,
    stem_weight_hbm,
    conv_gain_hbm,
    dilated_hbm,
    widen_hbm,
    token_gain_hbm,
    proj_hbm,
    pair_one_hbm,
    pair_two_hbm,
    stem_ref,
    normed_ref,
    taps_ref,
    edge_weight_ref,
    stem_weight_ref,
    conv_gain_ref,
    widen_ref,
    token_gain_ref,
    proj_ref,
    pair_one_ref,
    pair_two_ref,
    codes_ref,
    near_ref,
    dilated_ref,
    sum_ref,
    sems,
):
    copies = [
        pltpu.make_async_copy(source, target, sems.at[n])
        for n, (source, target) in enumerate(
            (
                (codes_hbm, codes_ref),
                (stem_weight_hbm, stem_weight_ref),
                (conv_gain_hbm, conv_gain_ref),
                (dilated_hbm, dilated_ref),
                (widen_hbm, widen_ref),
                (token_gain_hbm, token_gain_ref),
                (proj_hbm, proj_ref),
                (pair_one_hbm, pair_one_ref),
                (pair_two_hbm, pair_two_ref),
            )
        )
    ]
    for copy in copies:
        copy.start()
    core = place_ref[0]
    code_rows = codes_ref.shape[0] // 2
    rows = code_rows * SUB
    ext = rows + 2 * SUB
    for copy in copies[:3]:
        copy.wait()
    own = jnp.where(core == 0, codes_ref[:code_rows], codes_ref[code_rows:])
    near_ref[SUB : SUB + code_rows] = own
    near_ref[0:SUB] = codes_ref[code_rows - SUB : code_rows]
    near_ref[SUB + code_rows : 2 * SUB + code_rows] = codes_ref[code_rows : code_rows + SUB]
    tiles = [
        near_ref[pl.ds(SUB - 1 + r, SUB, stride=0), :] for r in range(code_rows + 2)
    ]
    row = iota((ext, 4 * PATCH), 0)
    valid = ((row >= SUB) | (core > 0)) & ((row < ext - SUB) | (core == 0))
    stem, normed = stem_of(
        spread_codes(tiles), valid, stem_weight_ref[...], in_lanes(conv_gain_ref[...])
    )
    stem_ref[...] = stem[SUB : SUB + rows].astype(jnp.bfloat16)
    normed_ref[...] = normed
    copies[3].wait()
    taps_ref[...] = taps_of(normed, dilated_ref, sum_ref, rows, slice(0, dilated_ref.shape[2]))
    edge_weight_ref[...] = dilated_ref[2 * core]
    for copy in copies[4:]:
        copy.wait()


def stem_call(place, codes, stem_weight, conv_gain, dilated, widen, token_gain, proj, one, two):
    channels = stem_weight.shape[1]
    half = dilated.shape[2]
    rows = codes.shape[0] // 2 * SUB
    shape = jax.ShapeDtypeStruct
    out_shape = (
        shape((rows, channels), jnp.bfloat16),
        shape((rows + 2 * SUB, channels), jnp.bfloat16),
        shape((rows, half), jnp.float32),
        shape((channels, half), jnp.bfloat16),
        shape(stem_weight.shape, jnp.bfloat16),
        shape(conv_gain.shape, jnp.float32),
        shape(widen.shape, jnp.bfloat16),
        shape(token_gain.shape, jnp.float32),
        shape(proj.shape, jnp.bfloat16),
        shape(one.shape, jnp.bfloat16),
        shape(two.shape, jnp.bfloat16),
    )
    return pl.pallas_call(
        stem_kernel,
        out_shape=out_shape,
        in_specs=[SMEM] + [HBM] * 9,
        out_specs=(VMEM,) * len(out_shape),
        scratch_shapes=[
            pltpu.VMEM(codes.shape, jnp.int32),
            pltpu.VMEM((codes.shape[0] // 2 + 3 * SUB, LANES), jnp.int32),
            pltpu.VMEM(dilated.shape, jnp.bfloat16),
            pltpu.VMEM((rows + SUB, half), jnp.float32),
            pltpu.SemaphoreType.DMA((9,)),
        ],
        compiler_params=pltpu.CompilerParams(vmem_limit_bytes=LIMIT),
        cost_estimate=pl.CostEstimate(
            flops=6 * rows * channels * half, bytes_accessed=4 << 20, transcendentals=0
        ),
        name="stem",
    )(place, codes, stem_weight, conv_gain, dilated, widen, token_gain, proj, one, two)


def tower_kernel(
    place_ref,
    received_ref,
    stem_ref,
    normed_ref,
    taps_ref,
    edge_weight_ref,
    stem_weight_ref,
    conv_gain_ref,
    dilated_ref,
    halved_ref,
    near_ref,
    sum_ref,
    tower_ref,
):
    core, outside = place_ref[0], place_ref[1]
    rows = stem_ref.shape[0]
    end = received_ref.shape[0]
    near_ref[0:SUB] = jnp.where(core == 0, received_ref[end - SUB :], received_ref[:SUB])
    near_ref[SUB:] = jnp.zeros((SUB, LANES), jnp.int32)
    tile = jnp.where(
        core == 0,
        near_ref[pl.ds(SUB - 1, SUB, stride=0), :],
        near_ref[pl.ds(0, SUB, stride=0), :],
    )
    normed = normed_ref[...]
    width = taps_ref.shape[1]
    chunks = [slice(0, width)]
    _, edge = stem_of(
        spread_codes([tile]), outside > 0, stem_weight_ref[...], in_lanes(conv_gain_ref[...])
    )

    parts = [taps_of(normed, dilated_ref, sum_ref, rows, chunk) for chunk in chunks]

    def finish(taps, added, which, first_column, slot):
        added = pltpu.roll(added, DILATION_ROWS, 0)
        row = iota(added.shape, 0)
        head = jnp.where((row < DILATION_ROWS) & (core == 0), added, 0.0)
        tail = jnp.where((row >= DILATION_ROWS) & (core > 0), added, 0.0)
        taps = jnp.concatenate(
            [taps[:SUB] + head, taps[SUB : rows - SUB], taps[rows - SUB :] + tail], axis=0
        )
        for c in range(0, taps.shape[1], LANES):
            start = pl.multiple_of(which * width + first_column + c, LANES)
            columns = pl.ds(start, LANES)
            stem = stem_ref[:, columns].astype(jnp.float32)
            slot_ref = tower_ref.at[slot + c // LANES]
            slot_ref[...] = stem + gelu_of(taps[:, c : c + LANES], 0.25)
            even = slot_ref[pl.ds(0, rows // 2, stride=2), :]
            odd = slot_ref[pl.ds(1, rows // 2, stride=2), :]
            halved_ref[:, columns] = jnp.maximum(even, odd).astype(jnp.bfloat16)

    finish(taps_ref[...], dot(edge, edge_weight_ref[...]), core, 0, 0)
    for part, chunk in zip(parts, chunks):
        added = dot(edge, dilated_ref[2 * core, :, chunk])
        finish(part, added, 1 - core, chunk.start, (width + chunk.start) // LANES)


def tower_call(place, received, stem, normed, taps, edge_weight, stem_weight, conv_gain, dilated):
    rows, channels = stem.shape
    half = taps.shape[1]
    return pl.pallas_call(
        tower_kernel,
        out_shape=jax.ShapeDtypeStruct((rows // 2, channels), jnp.bfloat16),
        in_specs=[SMEM] + [VMEM] * 8,
        out_specs=VMEM,
        scratch_shapes=[
            pltpu.VMEM((2 * SUB, LANES), jnp.int32),
            pltpu.VMEM((rows + SUB, half), jnp.float32),
            pltpu.VMEM((channels // LANES, rows, LANES), jnp.float32),
        ],
        compiler_params=pltpu.CompilerParams(vmem_limit_bytes=LIMIT),
        cost_estimate=pl.CostEstimate(
            flops=6 * rows * channels * half,
            bytes_accessed=4 << 20,
            transcendentals=rows * channels,
        ),
        name="tower",
    )(place, received, stem, normed, taps, edge_weight, stem_weight, conv_gain, dilated)


def widen_kernel(
    place_ref,
    halved_ref,
    widen_ref,
    widen_other_ref,
    token_gain_ref,
    proj_ref,
    fine_ref,
    fine_other_ref,
    spread_ref,
):
    core = place_ref[0]
    halved = halved_ref[...]
    token_count = halved.shape[0] // POOL
    wide = widen_ref.shape[1]
    gain = token_gain_ref[...]
    gain_rows = wide // LANES
    gains = [in_lanes(gain[:gain_rows]), in_lanes(gain[gain_rows:])]
    squares, factors = 0.0, 0.0
    for weight_ref, out_ref, which in (
        (widen_ref, fine_ref, core),
        (widen_other_ref, fine_other_ref, 1 - core),
    ):
        pieces = []
        for c in range(0, wide, 2 * LANES):
            columns = slice(c, c + 2 * LANES)
            fine = gelu_of(dot(halved, weight_ref[:, columns]), 0.5)
            out_ref[:, columns] = fine.astype(jnp.bfloat16)
            pieces.append(
                jnp.concatenate(
                    [
                        jnp.sum(fine[t * POOL : (t + 1) * POOL], axis=0, keepdims=True)
                        for t in range(token_count)
                    ],
                    axis=0,
                )
            )
        token = jnp.concatenate(pieces, axis=1) * (1.0 / POOL)
        token = token.astype(jnp.bfloat16).astype(jnp.float32)
        squares = squares + jnp.sum(token * token, axis=1, keepdims=True)
        start = pl.multiple_of(which * wide, LANES)
        scaled = (token * jnp.where(which == 0, gains[0], gains[1])).astype(jnp.bfloat16)
        factors = factors + dot(scaled, proj_ref[pl.ds(start, wide), :])
    factors = factors * lax.rsqrt(squares / (2 * wide) + epsilon)
    spread_ref[...] = jnp.broadcast_to(factors.astype(jnp.bfloat16)[None], spread_ref.shape)


def widen_call(place, halved, widen, widen_other, token_gain, proj, members):
    rows, channels = halved.shape
    wide = widen.shape[1]
    fine = jax.ShapeDtypeStruct((rows, wide), jnp.bfloat16)
    spread = jax.ShapeDtypeStruct((members, rows // POOL, 2 * PC), jnp.bfloat16)
    return pl.pallas_call(
        widen_kernel,
        out_shape=(fine, fine, spread),
        in_specs=[SMEM] + [VMEM] * 5,
        out_specs=(VMEM,) * 3,
        compiler_params=pltpu.CompilerParams(vmem_limit_bytes=LIMIT),
        cost_estimate=pl.CostEstimate(
            flops=4 * rows * channels * wide,
            bytes_accessed=4 << 20,
            transcendentals=2 * rows * wide,
        ),
        name="widen",
    )(place, halved, widen, widen_other, token_gain, proj)


def pair_kernel(
    tokens_total,
    height,
    width,
    place_ref,
    every_ref,
    dist_ref,
    weight_one_ref,
    weight_other_ref,
    weight_two_ref,
    fine_ref,
    fine_received_ref,
    fine_hbm,
    out_hbm,
    row_ref,
    col_ref,
    out_ref,
    sems,
):
    core, row_anchor, col_anchor = place_ref[0], place_ref[2], place_ref[3]
    fine_rows = fine_ref.shape[0]
    copies = []
    for n, (source, which) in enumerate(((fine_ref, core), (fine_received_ref, 1 - core))):
        start = pl.multiple_of(which * fine_rows, fine_rows)
        copies.append(
            pltpu.make_async_copy(source, fine_hbm.at[pl.ds(start, fine_rows)], sems.at[n])
        )
    for copy in copies:
        copy.start()
    per = every_ref.shape[1]
    members = tokens_total // per
    group_start = place_ref[4]
    cols = width + SUB
    high = height + 4
    for ref in (row_ref, col_ref):
        ref[0:SUB] = jnp.zeros((SUB, PC), jnp.float32)
        ref[tokens_total : tokens_total + 2 * SUB] = jnp.zeros((2 * SUB, PC), jnp.float32)
    for m in range(members):
        factors = every_ref[group_start + m].astype(jnp.float32)
        row_ref[2 + m * per : 2 + (m + 1) * per] = factors[:, :PC]
        col_ref[2 + m * per : 2 + (m + 1) * per] = factors[:, PC:]
    col_factor = col_ref[pl.ds(pl.multiple_of(col_anchor, SUB), cols), :]
    j = col_anchor - 2 + iota((cols, PC), 0)
    starts, masks = [], []
    for r in range(high):
        i = row_anchor - 2 + r
        row_factor = row_ref[pl.ds(row_anchor + r, SUB, stride=0), :]
        row_factor = jnp.concatenate([row_factor] * (cols // SUB), axis=0)
        distance = jnp.log1p(jnp.abs(i - j).astype(jnp.float32)) * (1.0 / math.log(tokens_total))
        starts.append(row_factor * col_factor + distance * dist_ref[...])
        masks.append(
            jnp.where((i >= 0) & (i < tokens_total) & (j >= 0) & (j < tokens_total), 1.0, 0.0)
        )
    start = jnp.concatenate(starts, axis=0).astype(jnp.bfloat16).astype(jnp.float32)
    mask = jnp.concatenate(masks, axis=0)

    def across(ref, a):
        return jnp.concatenate([ref[a, b] for b in range(3)], axis=1)

    def conv(active, first_ref, second_ref):
        weight = jnp.concatenate(
            [across(ref, a) for a in range(3) for ref in (first_ref, second_ref)], axis=0
        )
        size = active.shape[0]
        shifted = [active] + [pltpu.roll(active, size - b, 0) for b in (1, 2)]
        wide = jnp.concatenate([s.astype(jnp.bfloat16) for s in shifted], axis=1)
        taps = lax.dot_general(
            wide, weight, (((1,), (1,)), ((), ())), preferred_element_type=jnp.float32
        )
        keep = size - 2 * cols
        return sum(taps[a * cols : a * cols + keep, a * PC : (a + 1) * PC] for a in range(3))

    size = high * cols
    centre = pltpu.roll(start, size - 1, 0)[cols : size - cols]
    centre_mask = pltpu.roll(mask, size - 1, 0)[cols : size - cols]
    added = conv(gelu(start) * mask, weight_one_ref, weight_other_ref)
    mid = centre + pltpu.roll(added, core * (PC // 2), 1)
    mid = mid.astype(jnp.bfloat16).astype(jnp.float32)
    result = conv(gelu(mid) * centre_mask, weight_two_ref, weight_two_ref)
    mid_size = mid.shape[0]
    mid_centre = pltpu.roll(mid, mid_size - 1, 0)[cols : mid_size - cols]
    own = pltpu.roll(mid_centre, core * (PC // 2), 1)
    result = result + own
    channels = out_ref.shape[2]
    for r in range(height):
        out_ref[r] = result[r * cols : r * cols + width, :channels].astype(jnp.bfloat16)
    copies.append(pltpu.make_async_copy(out_ref, out_hbm, sems.at[2]))
    copies[2].start()
    for copy in copies:
        copy.wait()


def pair_call(
    place,
    every,
    dist_weight,
    weight_one,
    weight_other,
    weight_two,
    fine,
    fine_received,
    tokens_total,
    height,
    width,
):
    channels = PC // 2
    rows, wide = fine.shape
    return pl.pallas_call(
        functools.partial(pair_kernel, tokens_total, height, width),
        out_shape=(
            jax.ShapeDtypeStruct((2 * rows, wide), jnp.bfloat16),
            jax.ShapeDtypeStruct((height, width, channels), jnp.bfloat16),
        ),
        in_specs=[SMEM] + [VMEM] * 7,
        out_specs=(HBM, HBM),
        scratch_shapes=[
            pltpu.VMEM((tokens_total + 2 * SUB, PC), jnp.float32),
            pltpu.VMEM((tokens_total + 2 * SUB, PC), jnp.float32),
            pltpu.VMEM((height, width, channels), jnp.bfloat16),
            pltpu.SemaphoreType.DMA((3,)),
        ],
        compiler_params=pltpu.CompilerParams(vmem_limit_bytes=32 << 20),
        name="pair",
    )(place, every, dist_weight, weight_one, weight_other, weight_two, fine, fine_received)


def per_device(
    base_codes,
    stem_weight,
    conv_gain,
    dilated_conv_weight,
    widen_weight,
    token_gain,
    proj_weight,
    dist_weight,
    pair_weight_one,
    pair_weight_two,
):
    seq_count = lax.axis_size("seq")
    section_count = lax.axis_size("section")
    core_count = lax.axis_size("chan")
    chip_count = seq_count * section_count
    members = chip_count * core_count
    group_count = lax.axis_size("groups")
    core = lax.axis_index("chan")
    chip = lax.axis_index(CHIPS)
    last = core_count - 1

    codes = base_codes.reshape(-1, LANES)
    pairs = []
    for g in range(group_count):
        device = [(g * chip_count + i) * core_count for i in range(chip_count)]
        for low, high in zip(device[:-1], device[1:]):
            pairs += [(low + last, high), (high, low + last)]
        following = (g + 1) % group_count * members
        pairs += [(device[0], following), (device[-1] + last, following + members - 1)]
    received = lax.ppermute(codes, ALL, pairs)
    dilated_other = swap(dilated_conv_weight)
    widen_other = swap(widen_weight)
    in_hbm = functools.partial(pltpu.with_memory_space_constraint, memory_space=pltpu.HBM)
    pair_one = pair_weight_one.swapaxes(2, 3)
    pair_two = pair_weight_two.swapaxes(2, 3)
    pair_one_other = swap(pair_one)

    tokens_total = codes.shape[0] * LANES // PATCH // 2 // POOL * chip_count
    height = tokens_total // seq_count
    width = tokens_total // section_count
    place = jnp.stack(
        [
            core,
            jnp.where(core == 0, chip > 0, chip < chip_count - 1).astype(jnp.int32),
            lax.axis_index("seq") * height,
            lax.axis_index("section") * width,
            lax.axis_index("groups") * members,
        ]
    )
    gain_rows = conv_gain.reshape(-1, LANES)
    token_gain_rows = token_gain.reshape(-1, LANES)
    (
        stem,
        normed,
        taps,
        edge_weight,
        stem_weight,
        gain_rows,
        widen_own,
        token_gain_rows,
        proj,
        pair_one,
        pair_two,
    ) = stem_call(
        place,
        in_hbm(codes),
        in_hbm(stem_weight),
        in_hbm(gain_rows),
        in_hbm(dilated_conv_weight),
        in_hbm(widen_weight),
        in_hbm(token_gain_rows),
        in_hbm(proj_weight),
        in_hbm(pair_one),
        in_hbm(pair_two),
    )
    halved = tower_call(
        place, received, stem, normed, taps, edge_weight, stem_weight, gain_rows, dilated_other
    )
    fine_own, fine_other, spread = widen_call(
        place, halved, widen_own, widen_other, token_gain_rows, proj, group_count * members
    )
    fine_received = swap(fine_other)
    every = lax.all_to_all(spread, ALL, 0, 0, tiled=True)
    fine_features, pair_map = pair_call(
        place,
        every,
        dist_weight[None],
        pair_one,
        pair_one_other,
        pair_two,
        fine_own,
        fine_received,
        tokens_total,
        height,
        width,
    )
    return (fine_features, pair_map.transpose(2, 0, 1))


def solution(mesh):
    in_specs = (
        P(("groups", "seq", "section")),
        P(),
        P(),
        P(None, None, "chan"),
        P(None, "chan"),
        P(),
        P(),
        P(),
        P(None, None, None, "chan"),
        P(None, None, None, "chan"),
    )
    out_specs = (P(("groups", "seq", "section"), "chan"), P("chan", ("groups", "seq"), "section"))

    return jax.shard_map(
        per_device, mesh=mesh, in_specs=in_specs, out_specs=out_specs, check_vma=False
    )
```

```python
import functools
import math

import jax
import jax.numpy as jnp
from jax import lax
from jax.experimental import pallas as pl
from jax.experimental.pallas import tpu as pltpu
from jax.sharding import PartitionSpec as P


PC = 128
PATCH = 16
POOL = 64
DILATION_ROWS = 4


epsilon = 1e-06
LANES = 128
SUB = 8
CHIPS = ("seq", "section")
ALL = ("groups", "seq", "section", "chan")
VMEM = pl.BlockSpec(memory_space=pltpu.VMEM)
SMEM = pl.BlockSpec(memory_space=pltpu.SMEM)
HBM = pl.BlockSpec(memory_space=pltpu.HBM)
ANY = pl.BlockSpec(memory_space=pl.ANY)
LIMIT = 16 << 20
STEM_BLOCK = 96


def swap(values):
    count = lax.axis_size("chan")
    return lax.ppermute(values, "chan", [(i, count - 1 - i) for i in range(count)])


def dot(a, b):
    return jnp.dot(a, b, preferred_element_type=jnp.float32)


def gelu_of(part, share):
    linear = math.sqrt(2 / math.pi) / share
    cubic = 0.044715 * math.sqrt(2 / math.pi) / share**3
    return part + part * jnp.tanh(part * (linear + cubic * (part * part)))


def gelu(x):
    return gelu_of(0.5 * x, 0.5)


def iota(shape, axis):
    return lax.broadcasted_iota(jnp.int32, shape, axis)


def spread_codes(tiles):
    own_patch = iota((SUB, LANES), 1) // PATCH == iota((SUB, LANES), 0)
    picked = jnp.concatenate(
        [jnp.where(own_patch, t, 0).astype(jnp.float32) for t in tiles], axis=0
    ).astype(jnp.bfloat16)
    width = 4 * PATCH
    gather = (iota((LANES, width), 0) % PATCH == iota((LANES, width), 1) // 4).astype(jnp.bfloat16)
    return dot(picked, gather)


def stem_of(codes, valid, stem_weight, gain):
    base = (iota(codes.shape, 1) % 4).astype(jnp.float32)
    onehot = jnp.where((codes == base) & valid, 0.5, 0.0).astype(jnp.bfloat16)
    stem = dot(onehot, stem_weight)
    mean_square = jnp.mean(stem * stem, axis=1, keepdims=True)
    scale = 0.25 * lax.rsqrt(mean_square + 0.25 * epsilon)
    return stem, (stem * scale * gain).astype(jnp.bfloat16)


def in_lanes(rows):
    return jnp.concatenate([rows[r : r + 1] for r in range(rows.shape[0])], axis=1)


def taps_of(normed, weight_ref, sum_ref, rows, columns):
    first = dot(normed, weight_ref[0, :, columns])
    third = dot(normed, weight_ref[2, :, columns])
    centre = dot(normed, weight_ref[1, :, columns])
    sum_ref[:, columns] = first[: rows + SUB] + third[SUB:]
    return centre[SUB : SUB + rows] + sum_ref[DILATION_ROWS : DILATION_ROWS + rows, columns]


def stem_kernel(
    tokens_total,
    height,
    width,
    place_ref,
    codes_hbm,
    stem_weight_hbm,
    conv_gain_hbm,
    dilated_hbm,
    widen_hbm,
    token_gain_hbm,
    proj_hbm,
    pair_one_hbm,
    pair_two_hbm,
    stem_ref,
    normed_ref,
    taps_ref,
    edge_weight_ref,
    stem_weight_ref,
    conv_gain_ref,
    widen_ref,
    token_gain_ref,
    proj_ref,
    pair_one_ref,
    pair_two_ref,
    distance_ref,
    mask_ref,
    codes_ref,
    near_ref,
    dilated_ref,
    sum_ref,
    sems,
):
    core = place_ref[0]
    copies = [
        pltpu.make_async_copy(source, target, sems.at[n])
        for n, (source, target) in enumerate(
            (
                (codes_hbm, codes_ref),
                (stem_weight_hbm, stem_weight_ref),
                (conv_gain_hbm, conv_gain_ref),
                (dilated_hbm, dilated_ref),
                (dilated_hbm.at[2 * core], edge_weight_ref),
                (widen_hbm, widen_ref),
                (token_gain_hbm, token_gain_ref),
                (proj_hbm, proj_ref),
                (pair_one_hbm, pair_one_ref),
                (pair_two_hbm, pair_two_ref),
            )
        )
    ]
    for n, copy in enumerate(copies):
        copy.start(priority=int(n > 3))
    cols, high = width + SUB, height + 4
    for r in range(high):
        i = place_ref[2] - 2 + r
        j = place_ref[3] - 2 + iota((cols, PC), 0)
        inside = (i >= 0) & (i < tokens_total) & (j >= 0) & (j < tokens_total)
        gap = jnp.log1p(jnp.abs(i - j).astype(jnp.float32)) * (1.0 / math.log(tokens_total))
        distance_ref[r * cols : (r + 1) * cols] = jnp.where(inside, gap, 0.0)
        if 0 < r < high - 1:
            j += 1
            inside = (i >= 0) & (i < tokens_total) & (j >= 0) & (j < tokens_total)
            mask_ref[(r - 1) * cols : r * cols] = jnp.where(inside, 1.0, 0.0)
    code_rows = codes_ref.shape[0] // 2
    rows = code_rows * SUB
    ext = rows + 2 * SUB
    for copy in copies[:3]:
        copy.wait()
    own = jnp.where(core == 0, codes_ref[:code_rows], codes_ref[code_rows:])
    near_ref[SUB : SUB + code_rows] = own
    near_ref[0:SUB] = codes_ref[code_rows - SUB : code_rows]
    near_ref[SUB + code_rows : 2 * SUB + code_rows] = codes_ref[code_rows : code_rows + SUB]
    gain = in_lanes(conv_gain_ref[...])
    stem_weight = stem_weight_ref[...]
    block = STEM_BLOCK
    for first in range(0, ext, block):
        count = min(block, ext - first)
        tiles = [
            near_ref[pl.ds(SUB - 1 + r, SUB, stride=0), :]
            for r in range(first // SUB, (first + count) // SUB)
        ]
        row = first + iota((count, 4 * PATCH), 0)
        valid = ((row >= SUB) | (core > 0)) & ((row < ext - SUB) | (core == 0))
        stem, normed = stem_of(spread_codes(tiles), valid, stem_weight, gain)
        low, high = max(first, SUB), min(first + count, SUB + rows)
        stem_ref[low - SUB : high - SUB] = stem[low - first : high - first]
        normed_ref[first : first + count] = normed
    normed = normed_ref[...]
    copies[3].wait()
    taps_ref[...] = taps_of(normed, dilated_ref, sum_ref, rows, slice(0, dilated_ref.shape[2]))
    for copy in copies[4:]:
        copy.wait()


def stem_call(pair_sizes, place, codes, stem_weight, conv_gain, dilated, widen, token_gain, proj, one, two):
    channels = stem_weight.shape[1]
    half = dilated.shape[2]
    _, height, width = pair_sizes
    rows = codes.shape[0] // 2 * SUB
    shape = jax.ShapeDtypeStruct
    out_shape = (
        shape((rows, channels), jnp.float32),
        shape((rows + 2 * SUB, channels), jnp.bfloat16),
        shape((rows, half), jnp.float32),
        shape((channels, half), jnp.bfloat16),
        shape(stem_weight.shape, jnp.bfloat16),
        shape(conv_gain.shape, jnp.float32),
        shape(widen.shape, jnp.bfloat16),
        shape(token_gain.shape, jnp.float32),
        shape(proj.shape, jnp.bfloat16),
        shape(one.shape, jnp.bfloat16),
        shape(two.shape, jnp.bfloat16),
        shape(((height + 4) * (width + SUB), PC), jnp.float32),
        shape(((height + 2) * (width + SUB), PC), jnp.float32),
    )
    return pl.pallas_call(
        functools.partial(stem_kernel, *pair_sizes),
        out_shape=out_shape,
        in_specs=[SMEM] + [HBM] * 9,
        out_specs=(VMEM,) * len(out_shape),
        scratch_shapes=[
            pltpu.VMEM(codes.shape, jnp.int32),
            pltpu.VMEM((codes.shape[0] // 2 + 3 * SUB, LANES), jnp.int32),
            pltpu.VMEM(dilated.shape, jnp.bfloat16),
            pltpu.VMEM((rows + SUB, half), jnp.float32),
            pltpu.SemaphoreType.DMA((10,)),
        ],
        compiler_params=pltpu.CompilerParams(vmem_limit_bytes=LIMIT),
        cost_estimate=pl.CostEstimate(
            flops=6 * rows * channels * half, bytes_accessed=4 << 20, transcendentals=0
        ),
        name="stem",
    )(place, codes, stem_weight, conv_gain, dilated, widen, token_gain, proj, one, two)


def tower_kernel(
    place_ref,
    received_ref,
    stem_ref,
    normed_ref,
    taps_ref,
    edge_weight_ref,
    stem_weight_ref,
    conv_gain_ref,
    dilated_ref,
    halved_ref,
    near_ref,
    sum_ref,
    tower_ref,
):
    core, outside = place_ref[0], place_ref[1]
    rows = stem_ref.shape[0]
    end = received_ref.shape[0]
    near_ref[0:SUB] = jnp.where(core == 0, received_ref[end - SUB :], received_ref[:SUB])
    near_ref[SUB:] = jnp.zeros((SUB, LANES), jnp.int32)
    tile = jnp.where(
        core == 0,
        near_ref[pl.ds(SUB - 1, SUB, stride=0), :],
        near_ref[pl.ds(0, SUB, stride=0), :],
    )
    normed = normed_ref[...]
    width = taps_ref.shape[1]
    chunks = [slice(0, width)]
    _, edge = stem_of(
        spread_codes([tile]), outside > 0, stem_weight_ref[...], in_lanes(conv_gain_ref[...])
    )

    parts = [taps_of(normed, dilated_ref, sum_ref, rows, chunk) for chunk in chunks]

    def finish(taps, added, which, first_column, slot):
        added = pltpu.roll(added, DILATION_ROWS, 0)
        row = iota(added.shape, 0)
        head = jnp.where((row < DILATION_ROWS) & (core == 0), added, 0.0)
        tail = jnp.where((row >= DILATION_ROWS) & (core > 0), added, 0.0)
        taps = jnp.concatenate(
            [taps[:SUB] + head, taps[SUB : rows - SUB], taps[rows - SUB :] + tail], axis=0
        )
        for c in range(0, taps.shape[1], LANES):
            start = pl.multiple_of(which * width + first_column + c, LANES)
            columns = pl.ds(start, LANES)
            stem = stem_ref[:, columns]
            slot_ref = tower_ref.at[slot + c // LANES]
            slot_ref[...] = stem + gelu_of(taps[:, c : c + LANES], 0.25)
            even = slot_ref[pl.ds(0, rows // 2, stride=2), :]
            odd = slot_ref[pl.ds(1, rows // 2, stride=2), :]
            halved_ref[:, columns] = jnp.maximum(even, odd).astype(jnp.bfloat16)

    finish(taps_ref[...], dot(edge, edge_weight_ref[...]), core, 0, 0)
    for part, chunk in zip(parts, chunks):
        added = dot(edge, dilated_ref[2 * core, :, chunk])
        finish(part, added, 1 - core, chunk.start, (width + chunk.start) // LANES)


def tower_call(place, received, stem, normed, taps, edge_weight, stem_weight, conv_gain, dilated):
    rows, channels = stem.shape
    half = taps.shape[1]
    return pl.pallas_call(
        tower_kernel,
        out_shape=jax.ShapeDtypeStruct((rows // 2, channels), jnp.bfloat16),
        in_specs=[SMEM] + [VMEM] * 8,
        out_specs=VMEM,
        scratch_shapes=[
            pltpu.VMEM((2 * SUB, LANES), jnp.int32),
            pltpu.VMEM((rows + SUB, half), jnp.float32),
            pltpu.VMEM((channels // LANES, rows, LANES), jnp.float32),
        ],
        compiler_params=pltpu.CompilerParams(vmem_limit_bytes=LIMIT),
        cost_estimate=pl.CostEstimate(
            flops=6 * rows * channels * half,
            bytes_accessed=4 << 20,
            transcendentals=rows * channels,
        ),
        name="tower",
    )(place, received, stem, normed, taps, edge_weight, stem_weight, conv_gain, dilated)


def parcel_slots(weight_shape, fine_shape):
    across = fine_shape[1] // PC
    deep = -(-9 // across)
    return [(weight_shape[2] * (n // across), PC * (n % across)) for n in range(deep * across)]


def widen_kernel(
    place_ref,
    halved_ref,
    widen_ref,
    widen_other_ref,
    token_gain_ref,
    proj_ref,
    pair_one_ref,
    fine_ref,
    fine_other_ref,
    spread_ref,
):
    core = place_ref[0]
    halved = halved_ref[...]
    rows = halved.shape[0]
    for slot, (row, column) in enumerate(parcel_slots(pair_one_ref.shape, fine_other_ref.shape)):
        tap = min(slot, 8)
        part = pair_one_ref.shape[2]
        fine_other_ref[rows + row : rows + row + part, column : column + PC] = pair_one_ref[
            tap // 3, tap % 3
        ]
    token_count = halved.shape[0] // POOL
    wide = widen_ref.shape[1]
    gain = token_gain_ref[...]
    gain_rows = wide // LANES
    gains = [in_lanes(gain[:gain_rows]), in_lanes(gain[gain_rows:])]
    squares, factors = 0.0, 0.0
    for weight_ref, out_ref, which in (
        (widen_ref, fine_ref, core),
        (widen_other_ref, fine_other_ref, 1 - core),
    ):
        pieces = []
        for c in range(0, wide, 2 * LANES):
            columns = slice(c, c + 2 * LANES)
            fine = gelu_of(dot(halved, weight_ref[:, columns]), 0.5)
            out_ref[:rows, columns] = fine.astype(jnp.bfloat16)
            pieces.append(
                jnp.concatenate(
                    [
                        jnp.sum(fine[t * POOL : (t + 1) * POOL], axis=0, keepdims=True)
                        for t in range(token_count)
                    ],
                    axis=0,
                )
            )
        token = jnp.concatenate(pieces, axis=1) * (1.0 / POOL)
        token = token.astype(jnp.bfloat16).astype(jnp.float32)
        squares = squares + jnp.sum(token * token, axis=1, keepdims=True)
        start = pl.multiple_of(which * wide, LANES)
        scaled = (token * jnp.where(which == 0, gains[0], gains[1])).astype(jnp.bfloat16)
        factors = factors + dot(scaled, proj_ref[pl.ds(start, wide), :])
    factors = factors * lax.rsqrt(squares / (2 * wide) + epsilon)
    spread_ref[...] = jnp.broadcast_to(factors.astype(jnp.bfloat16)[None], spread_ref.shape)


def widen_call(place, halved, widen, widen_other, token_gain, proj, pair_one, members):
    rows, channels = halved.shape
    wide = widen.shape[1]
    fine = jax.ShapeDtypeStruct((rows, wide), jnp.bfloat16)
    below = parcel_slots(pair_one.shape, fine.shape)[-1][0] + pair_one.shape[2]
    parcel = jax.ShapeDtypeStruct((rows + below, wide), jnp.bfloat16)
    spread = jax.ShapeDtypeStruct((members, rows // POOL, 2 * PC), jnp.bfloat16)
    return pl.pallas_call(
        widen_kernel,
        out_shape=(fine, parcel, spread),
        in_specs=[SMEM] + [VMEM] * 6,
        out_specs=(VMEM,) * 3,
        compiler_params=pltpu.CompilerParams(vmem_limit_bytes=LIMIT),
        cost_estimate=pl.CostEstimate(
            flops=4 * rows * channels * wide,
            bytes_accessed=4 << 20,
            transcendentals=2 * rows * wide,
        ),
        name="widen",
    )(place, halved, widen, widen_other, token_gain, proj, pair_one)


def pair_kernel(
    tokens_total,
    height,
    width,
    place_ref,
    every_ref,
    dist_ref,
    distance_ref,
    mask_ref,
    weight_one_ref,
    weight_two_ref,
    fine_ref,
    fine_received_ref,
    fine_hbm,
    out_hbm,
    row_ref,
    col_ref,
    out_ref,
    sems,
):
    core, row_anchor, col_anchor = place_ref[0], place_ref[2], place_ref[3]
    fine_rows = fine_ref.shape[0]
    copies = []
    for n, (source, which) in enumerate(
        ((fine_ref, core), (fine_received_ref.at[:fine_rows], 1 - core))
    ):
        start = pl.multiple_of(which * fine_rows, fine_rows)
        copies.append(
            pltpu.make_async_copy(source, fine_hbm.at[pl.ds(start, fine_rows)], sems.at[n])
        )
    for copy in copies:
        copy.start()
    per = every_ref.shape[1]
    members = tokens_total // per
    group_start = place_ref[4]
    cols = width + SUB
    high = height + 4
    for ref in (row_ref, col_ref):
        ref[0:SUB] = jnp.zeros((SUB, PC), jnp.float32)
        ref[tokens_total : tokens_total + 2 * SUB] = jnp.zeros((2 * SUB, PC), jnp.float32)
    for m in range(members):
        factors = every_ref[group_start + m].astype(jnp.float32)
        row_ref[2 + m * per : 2 + (m + 1) * per] = factors[:, :PC]
        col_ref[2 + m * per : 2 + (m + 1) * per] = factors[:, PC:]
    col_factor = col_ref[pl.ds(pl.multiple_of(col_anchor, SUB), cols), :]
    starts = []
    for r in range(high):
        row_factor = row_ref[pl.ds(row_anchor + r, SUB, stride=0), :]
        row_factor = jnp.concatenate([row_factor] * (cols // SUB), axis=0)
        distance = distance_ref[r * cols : (r + 1) * cols]
        starts.append(row_factor * col_factor + distance * dist_ref[...])
    start = jnp.concatenate(starts, axis=0).astype(jnp.bfloat16).astype(jnp.float32)

    part = weight_one_ref.shape[2]
    slots = parcel_slots(weight_one_ref.shape, fine_received_ref.shape)

    def received_tap(a, b):
        row, column = slots[3 * a + b]
        row += fine_rows
        return fine_received_ref[row : row + part, column : column + PC]

    def tap_of(ref):
        return lambda a, b: ref[a, b]

    def across(tap, a):
        return jnp.concatenate([tap(a, b) for b in range(3)], axis=1)

    def conv(active, first, second):
        weight = jnp.concatenate(
            [across(tap, a) for a in range(3) for tap in (first, second)], axis=0
        )
        size = active.shape[0]
        shifted = [active] + [pltpu.roll(active, size - b, 0) for b in (1, 2)]
        wide = jnp.concatenate([s.astype(jnp.bfloat16) for s in shifted], axis=1)
        taps = lax.dot_general(
            wide, weight, (((1,), (1,)), ((), ())), preferred_element_type=jnp.float32
        )
        keep = size - 2 * cols
        return sum(taps[a * cols : a * cols + keep, a * PC : (a + 1) * PC] for a in range(3))

    size = high * cols
    centre = pltpu.roll(start, size - 1, 0)[cols : size - cols]
    added = conv(gelu(start), tap_of(weight_one_ref), received_tap)
    mid = centre + pltpu.roll(added, core * (PC // 2), 1)
    mid = mid.astype(jnp.bfloat16).astype(jnp.float32)
    result = conv(gelu(mid) * mask_ref[...], tap_of(weight_two_ref), tap_of(weight_two_ref))
    mid_size = mid.shape[0]
    mid_centre = pltpu.roll(mid, mid_size - 1, 0)[cols : mid_size - cols]
    own = pltpu.roll(mid_centre, core * (PC // 2), 1)
    result = result + own
    channels = out_ref.shape[2]
    for r in range(height):
        out_ref[r] = result[r * cols : r * cols + width, :channels].astype(jnp.bfloat16)
    copies.append(pltpu.make_async_copy(out_ref, out_hbm, sems.at[2]))
    copies[2].start()
    for copy in copies:
        copy.wait()


def pair_call(
    place,
    every,
    dist_weight,
    distance,
    mask,
    weight_one,
    weight_two,
    fine,
    fine_received,
    tokens_total,
    height,
    width,
):
    channels = PC // 2
    rows, wide = fine.shape
    return pl.pallas_call(
        functools.partial(pair_kernel, tokens_total, height, width),
        out_shape=(
            jax.ShapeDtypeStruct((2 * rows, wide), jnp.bfloat16),
            jax.ShapeDtypeStruct((height, width, channels), jnp.bfloat16),
        ),
        in_specs=[SMEM] + [VMEM] * 8,
        out_specs=(HBM, HBM),
        scratch_shapes=[
            pltpu.VMEM((tokens_total + 2 * SUB, PC), jnp.float32),
            pltpu.VMEM((tokens_total + 2 * SUB, PC), jnp.float32),
            pltpu.VMEM((height, width, channels), jnp.bfloat16),
            pltpu.SemaphoreType.DMA((3,)),
        ],
        compiler_params=pltpu.CompilerParams(vmem_limit_bytes=32 << 20),
        name="pair",
    )(place, every, dist_weight, distance, mask, weight_one, weight_two, fine, fine_received)


def per_device(
    base_codes,
    stem_weight,
    conv_gain,
    dilated_conv_weight,
    widen_weight,
    token_gain,
    proj_weight,
    dist_weight,
    pair_weight_one,
    pair_weight_two,
):
    seq_count = lax.axis_size("seq")
    section_count = lax.axis_size("section")
    core_count = lax.axis_size("chan")
    chip_count = seq_count * section_count
    members = chip_count * core_count
    group_count = lax.axis_size("groups")
    core = lax.axis_index("chan")
    chip = lax.axis_index(CHIPS)
    last = core_count - 1

    codes = base_codes.reshape(-1, LANES)
    pairs = []
    for g in range(group_count):
        device = [(g * chip_count + i) * core_count for i in range(chip_count)]
        for low, high in zip(device[:-1], device[1:]):
            pairs += [(low + last, high), (high, low + last)]
        following = (g + 1) % group_count * members
        pairs += [(device[0], following), (device[-1] + last, following + members - 1)]
    received = lax.ppermute(codes, ALL, pairs)
    dilated_other = swap(dilated_conv_weight)
    widen_other = swap(widen_weight)
    in_hbm = functools.partial(pltpu.with_memory_space_constraint, memory_space=pltpu.HBM)
    pair_one = pair_weight_one.swapaxes(2, 3)
    pair_two = pair_weight_two.swapaxes(2, 3)

    tokens_total = codes.shape[0] * LANES // PATCH // 2 // POOL * chip_count
    height = tokens_total // seq_count
    width = tokens_total // section_count
    place = jnp.stack(
        [
            core,
            jnp.where(core == 0, chip > 0, chip < chip_count - 1).astype(jnp.int32),
            lax.axis_index("seq") * height,
            lax.axis_index("section") * width,
            lax.axis_index("groups") * members,
        ]
    )
    gain_rows = conv_gain.reshape(-1, LANES)
    token_gain_rows = token_gain.reshape(-1, LANES)
    (
        stem,
        normed,
        taps,
        edge_weight,
        stem_weight,
        gain_rows,
        widen_own,
        token_gain_rows,
        proj,
        pair_one,
        pair_two,
        distance,
        mask,
    ) = stem_call(
        (tokens_total, height, width),
        place,
        in_hbm(codes),
        in_hbm(stem_weight),
        in_hbm(gain_rows),
        in_hbm(dilated_conv_weight),
        in_hbm(widen_weight),
        in_hbm(token_gain_rows),
        in_hbm(proj_weight),
        in_hbm(pair_one),
        in_hbm(pair_two),
    )
    halved = tower_call(
        place, received, stem, normed, taps, edge_weight, stem_weight, gain_rows, dilated_other
    )
    fine_own, fine_other, spread = widen_call(
        place, halved, widen_own, widen_other, token_gain_rows, proj, pair_one, group_count * members
    )
    fine_received = swap(fine_other)
    every = lax.all_to_all(spread, ALL, 0, 0, tiled=True)
    fine_features, pair_map = pair_call(
        place,
        every,
        dist_weight[None],
        distance,
        mask,
        pair_one,
        pair_two,
        fine_own,
        fine_received,
        tokens_total,
        height,
        width,
    )
    return (fine_features, pair_map.transpose(2, 0, 1))


def solution(mesh):
    in_specs = (
        P(("groups", "seq", "section")),
        P(),
        P(),
        P(None, None, "chan"),
        P(None, "chan"),
        P(),
        P(),
        P(),
        P(None, None, None, "chan"),
        P(None, None, None, "chan"),
    )
    out_specs = (P(("groups", "seq", "section"), "chan"), P("chan", ("groups", "seq"), "section"))

    return jax.shard_map(
        per_device, mesh=mesh, in_specs=in_specs, out_specs=out_specs, check_vma=False
    )
```
